32 devices in a mesh: dp: 32 (over z, y, x, core).
Axes of the slice: x: 2, y: 2, z: 4, core: 2. Of those that a mesh axis runs over, the one named last changes fastest.
Arguments:
- tokens: bfloat16 [32, 1024, 768], P('dp'), may hold values from -6 to 6
- prompt: float32 [50, 768], replicated, may hold values from -6 to 6
- segment_ids: int32 [32, 1024], P('dp'), may hold values from 0 to 4, as said below
- pad_flags: int32 [32, 1024], P('dp'), may hold values from 0 to 1, as said below
- prompt_slots: int32 [32, 1024], P('dp'), may hold values from 0 to 50, as said below
- first_gain: float32 [768], replicated, may hold values from 0.5 to 1.5
- first_shift: float32 [768], replicated, may hold values from -1 to 1
- inproj_weight: bfloat16 [768, 2304], P('dp'), may hold values from -0.21875 to 0.21875
- inproj_bias: float32 [2304], replicated, may hold values from -1.5 to 1.5
- outproj_weight: bfloat16 [768, 768], P('dp'), may hold values from -0.875 to 0.875
- outproj_bias: float32 [768], replicated, may hold values from -1.5 to 1.5
- second_gain: float32 [768], replicated, may hold values from 0.5 to 1.5
- second_shift: float32 [768], replicated, may hold values from -1 to 1
- expand_weight: bfloat16 [768, 3072], P('dp'), may hold values from -0.21875 to 0.21875
- expand_bias: float32 [3072], replicated, may hold values from -1.5 to 1.5
- reduce_weight: bfloat16 [3072, 768], P('dp'), may hold values from -0.109375 to 0.109375
- reduce_bias: float32 [768], replicated, may hold values from -1.5 to 1.5
- cotangent: bfloat16 [32, 1024, 768], P('dp'), may hold values from -6 to 6
Outputs:
- output: bfloat16 [32, 1024, 768], P('dp')
- grad_tokens: bfloat16 [32, 1024, 768], P('dp')
- grad_prompt: float32 [50, 768], replicated
The draws below stay inside these ranges and needn't reach their ends.
Inputs may be any that keep to these rules, and one draw needn't show every extreme that they name: `segment_ids`: each row holds 4 images, numbered 0 to 3 in the row's order, each on 247 consecutive slots; every other slot has the id 4. `pad_flags`: 1 exactly at the slots whose segment id is 4. `prompt_slots`: each image holds every prompt index 0 to 49 at exactly one of its slots; all other slots hold 50.
All inputs are finite; a program needn't handle non-finite values.
Results may differ from the reference program's by a relative error of at most 0.012.
Values may be sent and summed in bfloat16 or wider, within the bound.
A program may use at most 128 MiB of HBM per device.

```python
import jax
import jax.numpy as jnp
from jax import lax

D = 768
HEADS = 12
HEAD_DIM = 64
FF = 3072
PROMPTS = 50
PATCHES = 196
IMAGES_ROW = 4
SEQ = 1024
ROWS = 32


def layout(key):
    base_key = jax.random.fold_in(key, 4711)
    image_tokens = 1 + PROMPTS + PATCHES
    unit_count = IMAGES_ROW + SEQ - IMAGES_ROW * image_tokens
    row_keys = jax.random.split(base_key, 2 * ROWS)

    def one_row(order_key, role_key):
        ordering = jax.random.permutation(order_key, unit_count).astype(jnp.int32)
        is_image = (ordering < IMAGES_ROW).astype(jnp.int32)
        unit_length = jnp.where(is_image == 1, image_tokens, 1).astype(jnp.int32)
        unit_ends = jnp.cumsum(unit_length).astype(jnp.int32)
        unit_starts = unit_ends - unit_length
        position = jnp.arange(SEQ, dtype=jnp.int32)
        token_unit = jnp.sum((unit_starts[None, :] <= position[:, None]).astype(jnp.int32), axis=1) - 1
        image_number = (jnp.cumsum(is_image) - 1).astype(jnp.int32)
        unit_image = is_image[token_unit]
        image_index = jnp.clip(image_number[token_unit], 0, IMAGES_ROW - 1)
        token_offset = jnp.clip(position - unit_starts[token_unit], 0, image_tokens - 1)
        role_keys = jax.random.split(role_key, IMAGES_ROW)
        role_table = jax.vmap(lambda one_key: jax.random.permutation(one_key, image_tokens).astype(jnp.int32))(role_keys)
        token_role = role_table[image_index, token_offset]
        segment_id = jnp.where(unit_image == 1, image_index, IMAGES_ROW).astype(jnp.int32)
        pad_flag = (1 - unit_image).astype(jnp.int32)
        is_prompt = (unit_image == 1) & (token_role >= 1) & (token_role <= PROMPTS)
        prompt_slot = jnp.where(is_prompt, token_role - 1, PROMPTS).astype(jnp.int32)
        return (segment_id, pad_flag, prompt_slot)
    return jax.vmap(one_row)(row_keys[:ROWS], row_keys[ROWS:])


def draw_segment_ids(key, part):
    return layout(key)[0]


def draw_pad_flags(key, part):
    return layout(key)[1]


def draw_prompt_slots(key, part):
    return layout(key)[2]


def steps_of(stream_key, dims, cuts, least, top_value):
    def one(dim, shards_of):
        steps = jax.random.uniform(jax.random.fold_in(jax.random.fold_in(stream_key, 6), dim), (shards_of,), jnp.float32, least / len(cuts), top_value / len(cuts))
        return jnp.repeat(jnp.exp(steps), dims[dim] // shards_of).reshape((-1,) + (1,) * (len(dims) - dim - 1))

    loudness = one(*cuts[0])
    for cut in cuts[1:]:
        loudness = loudness * one(*cut)
    return loudness


def normal_values(key, extent, width, most, pieces=(), kind=jnp.bfloat16):
    entries = jax.random.normal(key, extent, jnp.float32) * width
    if len(pieces) > 0:
        entries = steps_of(key, extent, pieces, -0.22, 0.18) * entries
    return jnp.clip(entries, min=-most, max=most).astype(kind)


def setup_inputs(seed: int = 0) -> dict:
    key_of = jax.random.split(jax.random.key(seed), 19)
    return {
        "tokens": normal_values(key_of[0], (ROWS, SEQ, D), 1.0, 6.0, ((0, 32),)),
        "prompt": normal_values(key_of[1], (PROMPTS, D), 1.0, 6.0, (), jnp.float32),
        "segment_ids": draw_segment_ids(jax.random.fold_in(key_of[18], 71), 0),
        "pad_flags": draw_pad_flags(jax.random.fold_in(key_of[18], 71), 0),
        "prompt_slots": draw_prompt_slots(jax.random.fold_in(key_of[18], 71), 0),
        "first_gain": jnp.clip(1.0 + 0.1 * jax.random.normal(key_of[5], (D,), jnp.float32), 0.5, 1.5),
        "first_shift": normal_values(key_of[6], (D,), 0.2, 1.0, (), jnp.float32),
        "inproj_weight": normal_values(key_of[7], (D, 3 * D), D ** -0.5, 0.21875, ((0, 32),)),
        "inproj_bias": normal_values(key_of[8], (3 * D,), 0.3, 1.5, (), jnp.float32),
        "outproj_weight": normal_values(key_of[9], (D, D), (D // 16) ** -0.5, 0.875, ((0, 32),)),
        "outproj_bias": normal_values(key_of[10], (D,), 0.3, 1.5, (), jnp.float32),
        "second_gain": jnp.clip(1.0 + 0.1 * jax.random.normal(key_of[11], (D,), jnp.float32), 0.5, 1.5),
        "second_shift": normal_values(key_of[12], (D,), 0.2, 1.0, (), jnp.float32),
        "expand_weight": normal_values(key_of[13], (D, FF), D ** -0.5, 0.21875, ((0, 32),)),
        "expand_bias": normal_values(key_of[14], (FF,), 0.3, 1.5, (), jnp.float32),
        "reduce_weight": normal_values(key_of[15], (FF, D), FF ** -0.5, 0.109375, ((0, 32),)),
        "reduce_bias": normal_values(key_of[16], (D,), 0.3, 1.5, (), jnp.float32),
        "cotangent": normal_values(key_of[17], (ROWS, SEQ, D), 1.0, 6.0, ((0, 32),)),
    }


highest = lax.Precision.HIGHEST
eps = 1e-06
big_negative = -1e+30

@jax.custom_vjp
def low(v):
    return lax.optimization_barrier(v.astype(jnp.bfloat16)).astype(jnp.float32)

@jax.custom_vjp
def low_back(v):
    return v

def low_keep(v):
    return (low(v), None)

def low_pass(kept, grad):
    return (grad,)

def back_keep(v):
    return (v, None)

def back_low(kept, grad):
    return (low(grad),)
low.defvjp(low_keep, low_pass)
low_back.defvjp(back_keep, back_low)

def normalize(hidden_state, gain, shift):
    row_mean = lax.optimization_barrier(jnp.mean(hidden_state, axis=-1, keepdims=True))
    centered = hidden_state - row_mean
    variance = lax.optimization_barrier(jnp.mean(centered * centered, axis=-1, keepdims=True))
    return centered * lax.rsqrt(variance + eps) * gain + shift

def row_layer(row_input, prompt_input, slots, segments, frozen):
    first_gain, first_shift, inproj_weight, inproj_bias, outproj_weight, outproj_bias, second_gain, second_shift, expand_weight, expand_bias, reduce_weight, reduce_bias = frozen
    seq_len = row_input.shape[0]
    onehot = (slots[:, None] == jnp.arange(PROMPTS, dtype=jnp.int32)[None, :]).astype(jnp.float32)
    placed = jnp.dot(onehot, prompt_input, precision=highest)
    start = jnp.where((slots < PROMPTS)[:, None], placed, row_input)
    first = low(normalize(start, first_gain, first_shift))
    qkv = low_back(low(jnp.dot(first, inproj_weight, precision=highest) + inproj_bias))
    split_heads = qkv.reshape(seq_len, 3, HEADS, HEAD_DIM)
    head_query = split_heads[:, 0]
    head_key = split_heads[:, 1]
    head_value = split_heads[:, 2]
    scores = low_back(jnp.einsum('qhd,khd->hqk', head_query, head_key, precision=highest) * (1.0 / HEAD_DIM ** 0.5))
    same_image = segments[:, None] == segments[None, :]
    scores = jnp.where(same_image[None], scores, big_negative)
    row_max = lax.optimization_barrier(jnp.max(scores, axis=-1, keepdims=True))
    weights = jnp.exp(scores - row_max)
    probs = low(weights / lax.optimization_barrier(jnp.sum(weights, axis=-1, keepdims=True)))
    mixed = jnp.einsum('hqk,khd->qhd', probs, head_value, precision=highest).reshape(seq_len, HEADS * HEAD_DIM)
    mixed = low_back(low(mixed))
    middle = start + low_back(jnp.dot(mixed, outproj_weight, precision=highest) + outproj_bias)
    second = low(normalize(middle, second_gain, second_shift))
    pre = low_back(jnp.dot(second, expand_weight, precision=highest) + expand_bias)
    hidden = low(jax.nn.gelu(pre, approximate=False))
    return middle + low_back(jnp.dot(hidden, reduce_weight, precision=highest) + reduce_bias)

def reference(tokens, prompt, segment_ids, pad_flags, prompt_slots, first_gain, first_shift, inproj_weight, inproj_bias, outproj_weight, outproj_bias, second_gain, second_shift, expand_weight, expand_bias, reduce_weight, reduce_bias, cotangent):
    frozen = tuple((param.astype(jnp.float32) for param in (first_gain, first_shift, inproj_weight, inproj_bias, outproj_weight, outproj_bias, second_gain, second_shift, expand_weight, expand_bias, reduce_weight, reduce_bias)))
    prompt_float = prompt.astype(jnp.float32)

    def one_row(prompt_total, row_inputs):
        row_tokens, slots, segments, pads, row_cot = row_inputs

        def layer(row_input, prompt_input):
            return row_layer(row_input, prompt_input, slots, segments, frozen)
        row_output, pullback = jax.vjp(layer, row_tokens.astype(jnp.float32), prompt_float)
        live_mask = (1 - pads).astype(jnp.float32)[:, None]
        grad_row, grad_part = pullback(row_cot.astype(jnp.float32) * live_mask)
        return (prompt_total + grad_part, (row_output.astype(jnp.bfloat16), grad_row.astype(jnp.bfloat16)))
    prompt_total, (outputs, grads) = lax.scan(one_row, jnp.zeros((PROMPTS, D), jnp.float32), (tokens, prompt_slots, segment_ids, pad_flags, cotangent))
    return (outputs, grads, prompt_total)
```

```python
import functools

import jax
import jax.numpy as jnp
from jax import lax
from jax.experimental import pallas as pl
from jax.experimental.pallas import tpu as pltpu
from jax.sharding import PartitionSpec as P

HEADS = 12
HEAD_DIM = 64
PROMPTS = 50
PATCHES = 196
IMAGES = 4
IMAGE_SLOTS = 1 + PROMPTS + PATCHES
EPS = 1e-06
BIG_NEGATIVE = -1e30
MESH = pl.DeviceIdType.MESH
F32 = jnp.float32
BF16 = jnp.bfloat16
DIMS = (4, 2, 2, 2)
VMEM_LIMIT = 67043328

ERF_C = 0.39
ERF_P = (0.15142707, 0.1944365, -0.01663455, 0.37516693, -0.25824265, 0.0538467)


def dot(a, b):
    return jnp.dot(a, b, preferred_element_type=F32)


def dot_t(a, b):
    return lax.dot_general(a, b, (((1,), (1,)), ((), ())), preferred_element_type=F32)


def t_dot(a, b):
    return lax.dot_general(a, b, (((0,), (0,)), ((), ())), preferred_element_type=F32)


def gelu_both(x):
    a = jnp.abs(x)
    t = 1.0 / (1.0 + ERF_C * a)
    e = jnp.exp(x * x * -0.5)
    poly = ERF_P[5]
    for c in ERF_P[4::-1]:
        poly = poly * t + c
    q = poly * t * e
    phi = jnp.where(x >= 0.0, 1.0 - q, q)
    return x * phi, phi + x * e * 0.3989422804014327


class Gather:
    def __init__(self, srcs, dsts, rows, send_sem, recv_sem):
        Z, Y, X, C = DIMS
        self.src, self.dst, self.rows = srcs, dsts, rows
        self.send_sem, self.recv_sem = send_sem, recv_sem
        me = lax.axis_index("dp")
        self.me = me
        self.c = lax.rem(me, C)
        self.x = lax.rem(me // C, X)
        self.y = lax.rem(me // (C * X), Y)
        self.z = me // (C * X * Y)
        self.core = self.dev(self.z, self.y, self.x, 1 - self.c)
        self.xp = self.dev(self.z, self.y, 1 - self.x, self.c)
        self.yp = self.dev(self.z, 1 - self.y, self.x, self.c)
        self.dp = self.dev(self.z, 1 - self.y, 1 - self.x, self.c)
        self.zp = [self.dev(self.zo(j), self.y, self.x, self.c) for j in (1, 2, 3)]
        self.sent = [0] * len(rows)

    def dev(self, z, y, x, c):
        Z, Y, X, C = DIMS
        return ((z * Y + y) * X + x) * C + c

    def zo(self, j):
        return lax.rem(self.z + j, DIMS[0])

    def enter(self):
        barrier = pltpu.get_barrier_semaphore()
        peers = self.zp + [self.xp, self.yp, self.dp, self.core]
        for peer in peers:
            pl.semaphore_signal(barrier, inc=1, device_id=(peer,), device_id_type=MESH)
        pl.semaphore_wait(barrier, len(peers))

    def slot(self, k, owner):
        return self.dst[k].at[pl.ds(pl.multiple_of(owner * self.rows[k], 8), self.rows[k]), :]

    def copy(self, k, n, owner, to, src=None):
        slot = self.slot(k, owner)
        return pltpu.make_async_remote_copy(
            src_ref=slot if src is None else src,
            dst_ref=slot,
            send_sem=self.send_sem.at[k, n],
            recv_sem=self.recv_sem.at[k, owner],
            device_id=(to,),
            device_id_type=MESH,
        )

    def send(self, k, owner, to, src=None):
        self.copy(k, self.sent[k], owner, to, src).start()
        self.sent[k] += 1

    def wait(self, k, owner):
        self.copy(k, 0, owner, self.core).wait_recv()

    def line(self, k):
        for to in self.zp:
            self.send(k, self.me, to, self.src[k])

    def own(self, k):
        for to in (self.xp, self.yp, self.core):
            self.send(k, self.me, to, self.src[k])

    def column(self, k):
        for j in (1, 3, 2):
            owner = self.dev(self.zo(j), self.y, self.x, self.c)
            self.wait(k, owner)
            for to in (self.xp, self.yp, self.core):
                self.send(k, owner, to)

    def plane(self, k):
        for j in range(4):
            owner = self.dev(self.zo(j), self.y, 1 - self.x, self.c)
            self.wait(k, owner)
            if j < 2:
                self.send(k, owner, self.yp)
            self.send(k, owner, self.core)
            owner = self.dev(self.zo(j), 1 - self.y, self.x, self.c)
            self.wait(k, owner)
            if j >= 2:
                self.send(k, owner, self.xp)
            self.send(k, owner, self.core)

    def corner(self, k):
        for j in range(4):
            owner = self.dev(self.zo(j), 1 - self.y, 1 - self.x, self.c)
            self.wait(k, owner)
            self.send(k, owner, self.core)

    def arrive(self, k):
        @pl.loop(0, DIMS[0] * DIMS[1] * DIMS[2])
        def _(chip):
            self.wait(k, chip * DIMS[3] + 1 - self.c)

    def drain(self):
        for k, n in enumerate(self.sent):
            for i in range(n):
                self.copy(k, i, self.me, self.core).wait_send()


class Reduce:
    def __init__(self, g, acc, came, half, plane, line, total, sems):
        self.g, self.acc, self.came, self.half, self.plane, self.line, self.total = (
            g, acc, came, half, plane, line, total
        )
        self.send_sem, self.recv_sem = sems
        self.n = 0
        rows = acc.shape[0] // 8
        self.rows = rows
        self.mine = g.c * 4 + g.y * 2 + g.x

    def tile(self, ref, i):
        return ref.at[pl.ds(pl.multiple_of(i * self.rows, 8), self.rows), :]

    def exchange(self, moves):
        copies = []
        for src, dst, to in moves:
            copies.append(
                pltpu.make_async_remote_copy(
                    src_ref=src,
                    dst_ref=dst,
                    send_sem=self.send_sem.at[self.n],
                    recv_sem=self.recv_sem.at[self.n],
                    device_id=(to,),
                    device_id_type=MESH,
                )
            )
            self.n += 1
        for copy in copies:
            copy.start()
        return copies

    def steps(self):
        g, r = self.g, self.rows
        four = 4 * r

        def halves(ref, c):
            return ref.at[pl.ds(pl.multiple_of(c * four, 8), four), :]

        one = self.exchange([(halves(self.acc, 1 - g.c), self.came.at[:, :], g.core)])
        yield
        for copy in one:
            copy.wait()
        mine = pl.ds(pl.multiple_of(g.c * four, 8), four)
        self.half[:, :] = self.acc[mine, :] + self.came[:, :]
        moves = []
        for i, (dy, dx, to) in enumerate(((0, 1, g.xp), (1, 0, g.yp), (1, 1, g.dp))):
            y = g.y if dy == 0 else 1 - g.y
            x = g.x if dx == 0 else 1 - g.x
            moves.append((self.tile(self.half, y * 2 + x), self.plane.at[i], to))
        two = self.exchange(moves)
        yield
        for copy in two:
            copy.wait()
        own = pl.ds(pl.multiple_of((g.y * 2 + g.x) * r, 8), r)
        self.line[pl.ds(g.z, 1)] = (
            (self.half[own, :] + self.plane[0]) + (self.plane[1] + self.plane[2])
        )[None]
        three = self.exchange([(self.line.at[g.z], self.line.at[g.z], to) for to in g.zp])
        yield
        for copy in three:
            copy.wait()
        total = (self.line[0] + self.line[1]) + (self.line[2] + self.line[3])
        self.total[pl.ds(pl.multiple_of(self.mine * r, 8), r), :] = total
        mine_ref = self.tile(self.total, self.mine)
        four_c = self.exchange([(mine_ref, mine_ref, to) for to in (g.xp, g.yp, g.dp)])
        yield
        for copy in four_c:
            copy.wait()
        five = self.exchange([(halves(self.total, g.c), halves(self.total, g.c), g.core)])
        yield
        for copy in five:
            copy.wait()
        yield


def kernel(remote, shards, *refs):
    names = (
        "tokens", "prompt", "seg", "pads", "slots", "g1", "s1", "w1", "b1", "w2", "b2", "g2", "s2", "w3", "b3",
        "w4", "b4", "cot", "output", "grad_tokens", "grad_prompt", "W1", "W2", "W3", "W4", "perm", "start",
        "first", "qkv", "mixed", "middle", "second", "hidden", "slope", "probs", "gres", "gmid", "gmixed",
        "stats", "prompt_v", "seg_v", "pads_v", "slots_v", "g1_v", "s1_v", "b1_v", "b2_v", "g2_v", "s2_v",
        "b3_v", "b4_v", "acc", "came", "half", "plane", "line", "total", "in_sem", "loc_sem", "out_sem",
        "send_sem", "recv_sem", "rsend_sem", "rrecv_sem",
    )
    r = dict(zip(names, refs))
    seq, width = r["start"].shape
    block = seq // IMAGES
    pads_block = block - IMAGE_SLOTS
    ff = r["W3"].shape[1]
    pairs = HEADS // 2
    weights = [r["W1"], r["W2"], r["W3"], r["W4"]]

    def rows_of(b):
        return pl.ds(pl.multiple_of(b * block, block), block)

    small = []
    for i, name in enumerate(
        ("slots", "seg", "pads", "prompt", "g1", "s1", "b1", "b2", "g2", "s2", "b3", "b4")
    ):
        small.append(pltpu.make_async_copy(r[name], r[name + "_v"], r["in_sem"].at[i]))
    tok_in = pltpu.make_async_copy(r["tokens"].at[0], r["gmixed"], r["in_sem"].at[12])
    cot_in = pltpu.make_async_copy(r["cot"].at[0], r["mixed"], r["in_sem"].at[13])
    for copy in small + [tok_in, cot_in]:
        copy.start()
    srcs = [r["w1"], r["w2"], r["w3"], r["w4"]]
    if remote:
        g = Gather(srcs, weights, shards, r["send_sem"], r["recv_sem"])
        local = [pltpu.make_async_copy(srcs[k], g.slot(k, g.me), r["loc_sem"].at[k]) for k in range(4)]
    else:
        g = None
        local = [pltpu.make_async_copy(srcs[k], weights[k], r["loc_sem"].at[k]) for k in range(4)]
    for copy in local:
        copy.start()

    def comm(*words):
        if remote:
            for word in words:
                getattr(g, word[:-1])(int(word[-1]))

    def have(k):
        local[k].wait()
        if remote:
            g.arrive(k)

    if remote:
        g.enter()
    comm("line0", "own0", "line1", "line2", "line3", "own1", "own2", "own3")

    for copy in small:
        copy.wait()
    seg = r["seg_v"][...]
    slots = r["slots_v"][...]
    is_prompt = slots < PROMPTS
    group = jnp.where(is_prompt, -1, seg)
    wanted = lax.broadcasted_iota(jnp.int32, (8, seq), 0)
    member = (wanted == group).astype(F32)
    lane = 128
    before = (
        lax.broadcasted_iota(jnp.int32, (lane, lane), 0) < lax.broadcasted_iota(jnp.int32, (lane, lane), 1)
    ).astype(F32).astype(BF16)
    counts = []
    offset = jnp.zeros((8, 1), F32)
    for i in range(seq // lane):
        part = member[:, i * lane : (i + 1) * lane]
        counts.append(dot(part.astype(BF16), before) + offset)
        offset = offset + jnp.sum(part, axis=1, keepdims=True)
    rank = jnp.sum(jnp.concatenate(counts, axis=1) * member, axis=0, keepdims=True).astype(jnp.int32)
    part_of = jnp.zeros_like(rank)
    for i in range(1, IMAGES):
        part_of = part_of + (rank >= i * pads_block).astype(jnp.int32)
    pad_dest = part_of * block + IMAGE_SLOTS + (rank - part_of * pads_block)
    image_dest = seg * block + jnp.where(is_prompt, slots, PROMPTS + rank)
    dest = jnp.where(seg < IMAGES, image_dest, pad_dest)
    live_dest = jnp.where(r["pads_v"][...] == 0, dest, -1)

    def norm_stats(v):
        mean = jnp.mean(v, axis=-1, keepdims=True)
        centered = v - mean
        return centered, lax.rsqrt(jnp.mean(centered * centered, axis=-1, keepdims=True) + EPS), mean

    tok_in.wait()
    cot_in.wait()
    head_rows = -(-PROMPTS // 8) * 8

    def place(b, carry):
        rows = rows_of(b)
        row_id = lax.broadcasted_iota(jnp.int32, (block, seq), 0) + b * block
        one_hot = (row_id == dest).astype(F32).astype(BF16)
        x = dot(one_hot, r["gmixed"][...])
        r["start"][rows, :] = x
        r["start"][pl.ds(pl.multiple_of(b * block, block), PROMPTS), :] = r["prompt_v"][...]
        centered, rstd, mean = norm_stats(r["start"][rows, :])
        r["stats"][0, rows, :] = mean
        r["stats"][1, rows, :] = rstd
        r["first"][rows, :] = (centered * rstd * r["g1_v"][...] + r["s1_v"][...]).astype(BF16)
        live = (row_id == live_dest).astype(F32).astype(BF16)
        r["gres"][rows, :] = dot(live, r["mixed"][...]).astype(BF16)
        return carry

    lax.fori_loop(0, IMAGES, place, 0)
    dest_col = jnp.transpose(jnp.broadcast_to(dest.astype(F32), (8, seq)))[:, 0:1].astype(jnp.int32)
    r["stats"][4, :, :] = dest_col.astype(F32)

    def inverse(b, carry):
        rows = rows_of(b)
        col = r["stats"][4, rows, :].astype(jnp.int32)
        r["perm"][rows, :] = (lax.broadcasted_iota(jnp.int32, (block, seq), 1) == col).astype(F32).astype(BF16)
        return carry

    lax.fori_loop(0, IMAGES, inverse, 0)

    comm("column0", "column1", "plane0", "column2", "plane1", "corner0")
    have(0)

    scale = 1.0 / HEAD_DIM**0.5

    def project(b, carry):
        rows = rows_of(b)
        x = r["first"][rows, :]
        for i in range(3):
            cols = slice(i * width, (i + 1) * width)
            y = dot(x, r["W1"][:, cols]) + r["b1_v"][:, cols]
            y = y.astype(BF16)
            r["qkv"][rows, cols] = y * scale if i == 0 else y
        return carry

    lax.fori_loop(0, IMAGES, project, 0)
    comm("column3", "plane2", "corner1")

    lanes = 2 * HEAD_DIM

    def pair_cols(i, p):
        return pl.ds(pl.multiple_of(i * width + p * lanes, lanes), lanes)

    def masked(v, h):
        low = lax.broadcasted_iota(jnp.int32, v.shape, 1) < HEAD_DIM
        return jnp.where(low if h == 0 else jnp.logical_not(low), v, jnp.zeros_like(v))

    def soft(scores, allowed):
        scores = jnp.where(allowed, scores, BIG_NEGATIVE)
        e = jnp.exp(scores - jnp.max(scores, axis=-1, keepdims=True))
        return (e * (1.0 / jnp.sum(e, axis=-1, keepdims=True))).astype(BF16)

    def attend(i, carry):
        b, p = i // pairs, lax.rem(i, pairs)
        rows = rows_of(b)
        q, k, v = (r["qkv"][rows, pair_cols(j, p)] for j in range(3))
        in_image = lax.broadcasted_iota(jnp.int32, (block, block), 1) < IMAGE_SLOTS
        out = None
        for h in range(2):
            probs = soft(dot_t(masked(q, h), k), in_image)
            r["probs"][2 * i + h] = probs
            term = dot(probs, masked(v, h))
            out = term if out is None else out + term
        r["mixed"][rows, pair_cols(0, p)] = out.astype(BF16)
        return carry

    lax.fori_loop(0, IMAGES * pairs, attend, 0)

    tail = 16
    group_rows = IMAGES * tail

    def attend_pads(p, carry):
        def gathered(j):
            return jnp.concatenate(
                [
                    r["qkv"][b * block + block - tail : (b + 1) * block, pair_cols(j, p)]
                    for b in range(IMAGES)
                ],
                axis=0,
            )

        q, k, v = (gathered(j) for j in range(3))
        col = lax.rem(lax.broadcasted_iota(jnp.int32, (group_rows, group_rows), 1), tail)
        out = None
        for h in range(2):
            probs = soft(dot_t(masked(q, h), k), col >= tail - pads_block)
            term = dot(probs, masked(v, h))
            out = term if out is None else out + term
        out = out.astype(BF16)
        is_pad = lax.broadcasted_iota(jnp.int32, (tail, lanes), 0) >= tail - pads_block
        for b in range(IMAGES):
            where = slice(b * block + block - tail, (b + 1) * block)
            old = r["mixed"][where, pair_cols(0, p)]
            r["mixed"][where, pair_cols(0, p)] = jnp.where(is_pad, out[b * tail : (b + 1) * tail], old)
        return carry

    lax.fori_loop(0, pairs, attend_pads, 0)
    comm("plane3", "corner2")
    have(1)

    def join(b, carry):
        rows = rows_of(b)
        middle = r["start"][rows, :] + (dot(r["mixed"][rows, :], r["W2"][...]) + r["b2_v"][...])
        r["middle"][rows, :] = middle
        centered, rstd, mean = norm_stats(middle)
        r["stats"][2, rows, :] = mean
        r["stats"][3, rows, :] = rstd
        r["second"][rows, :] = (centered * rstd * r["g2_v"][...] + r["s2_v"][...]).astype(BF16)
        return carry

    lax.fori_loop(0, IMAGES, join, 0)
    have(2)
    parts = ff // width

    def expand(i, carry):
        b, n = i // parts, lax.rem(i, parts)
        rows = rows_of(b)
        cols = pl.ds(pl.multiple_of(n * width, width), width)
        pre = dot(r["second"][rows, :], r["W3"][:, cols]) + r["b3_v"][:, cols]
        hidden, slope = gelu_both(pre)
        r["hidden"][rows, cols] = hidden.astype(BF16)
        r["slope"][rows, cols] = slope.astype(BF16)
        return carry

    lax.fori_loop(0, IMAGES * parts, expand, 0)
    comm("corner3")
    have(3)

    def back_hidden(i, carry):
        b, n = i // parts, lax.rem(i, parts)
        rows = rows_of(b)
        cols = pl.ds(pl.multiple_of(n * width, width), width)
        grad = dot_t(r["gres"][rows, :], r["W4"][cols, :])
        r["slope"][rows, cols] = (grad * r["slope"][rows, cols].astype(F32)).astype(BF16)
        return carry

    lax.fori_loop(0, IMAGES * parts, back_hidden, 0)

    def norm_back(grad, v, mean, rstd, gain):
        unit = (v - mean) * rstd
        scaled = grad * gain
        first = jnp.mean(scaled, axis=-1, keepdims=True)
        second = jnp.mean(scaled * unit, axis=-1, keepdims=True)
        return rstd * (scaled - first - unit * second)

    def back_join(b, carry):
        rows = rows_of(b)
        grad = dot_t(r["slope"][rows, :], r["W3"][...])
        grad = norm_back(
            grad, r["middle"][rows, :], r["stats"][2, rows, :], r["stats"][3, rows, :], r["g2_v"][...]
        )
        grad = r["gres"][rows, :].astype(F32) + grad
        r["gmid"][rows, :] = grad
        r["gmixed"][rows, :] = dot_t(grad.astype(BF16), r["W2"][...]).astype(BF16)
        return carry

    lax.fori_loop(0, IMAGES, back_join, 0)

    def back_attend(i, carry):
        b, p = i // pairs, lax.rem(i, pairs)
        rows = rows_of(b)
        q, k, v = (r["qkv"][rows, pair_cols(j, p)] for j in range(3))
        grad_out = r["gmixed"][rows, pair_cols(0, p)]
        gq = gk = gv = None
        for h in range(2):
            probs = r["probs"][2 * i + h]
            go = masked(grad_out, h)
            dv = t_dot(probs, go)
            dp = dot_t(go, v)
            pf = probs.astype(F32)
            inner = jnp.sum(dp * pf, axis=-1, keepdims=True)
            ds = (pf * (dp - inner)).astype(BF16)
            dq = dot(ds, masked(k, h))
            dk = t_dot(ds, masked(q, h))
            gq, gk, gv = (dq, dk, dv) if h == 0 else (gq + dq, gk + dk, gv + dv)
        r["qkv"][rows, pair_cols(0, p)] = (gq * scale).astype(BF16)
        r["qkv"][rows, pair_cols(1, p)] = gk.astype(BF16)
        r["qkv"][rows, pair_cols(2, p)] = gv.astype(BF16)
        return carry

    lax.fori_loop(0, IMAGES * pairs, back_attend, 0)

    r["acc"][...] = jnp.zeros_like(r["acc"])
    heads_at = lax.broadcasted_iota(jnp.int32, (block, width), 0)

    def back_start(b, carry):
        rows = rows_of(b)
        grad = dot_t(r["qkv"][rows, :], r["W1"][...])
        grad = norm_back(
            grad, r["start"][rows, :], r["stats"][0, rows, :], r["stats"][1, rows, :], r["g1_v"][...]
        )
        grad = r["gmid"][rows, :] + grad
        top = grad[0:head_rows, :]
        keep = lax.broadcasted_iota(jnp.int32, (head_rows, width), 0) < PROMPTS
        r["acc"][0:head_rows, :] = r["acc"][0:head_rows, :] + jnp.where(keep, top, 0.0)
        r["second"][rows, :] = jnp.where(heads_at < PROMPTS, 0.0, grad).astype(BF16)
        return carry

    lax.fori_loop(0, IMAGES, back_start, 0)

    if remote:
        red = Reduce(
            g, *(r[name] for name in ("acc", "came", "half", "plane", "line", "total")), (r["rsend_sem"], r["rrecv_sem"])
        ).steps()
    else:
        r["total"][...] = r["acc"][...]
        red = iter(range(6))
    next(red)

    def reduce_out(b):
        rows = rows_of(b)
        y = r["middle"][rows, :] + (dot(r["hidden"][rows, :], r["W4"][...]) + r["b4_v"][...])
        r["first"][rows, :] = y.astype(BF16)

    def ship(b, src, stage, out, n):
        rows = rows_of(b)
        r[stage][rows, :] = dot(r["perm"][rows, :], r[src][...]).astype(BF16)
        pltpu.make_async_copy(r[stage].at[rows, :], r[out].at[0, rows, :], r["out_sem"].at[n, b]).start()

    for b in range(IMAGES):
        ship(b, "second", "gmixed", "grad_tokens", 0)
    next(red)
    reduce_out(0)
    next(red)
    reduce_out(1)
    reduce_out(2)
    next(red)
    reduce_out(3)
    next(red)
    for b in range(IMAGES):
        ship(b, "first", "mixed", "output", 1)
    next(red)
    r["grad_prompt"][...] = r["total"][0:PROMPTS, :]
    for n, (stage, out) in enumerate((("gmixed", "grad_tokens"), ("mixed", "output"))):
        for b in range(IMAGES):
            rows = slice(b * block, (b + 1) * block)
            pltpu.make_async_copy(r[stage].at[rows, :], r[out].at[0, rows, :], r["out_sem"].at[n, b]).wait()
    if remote:
        g.drain()


def layer(remote, shards, args, full):
    (tokens, prompt, seg, pads, slots, g1, s1, _, b1, _, b2, g2, s2, _, b3, _, b4, cot) = args
    w1, w2, w3, w4 = full
    _, seq, width = tokens.shape
    ff = b3.shape[0]
    mult = 32 if remote else 1
    row = lambda v: v.reshape(1, -1)
    operands = [
        tokens, prompt, seg, pads, slots, row(g1), row(s1), w1, row(b1), w2, row(b2), row(g2), row(s2),
        w3, row(b3), w4, row(b4), cot,
    ]
    acc_rows = 64
    dma = pltpu.SemaphoreType.DMA
    scratch = [
        pltpu.VMEM((w1.shape[0] * mult, 3 * width), BF16),
        pltpu.VMEM((w2.shape[0] * mult, width), BF16),
        pltpu.VMEM((w3.shape[0] * mult, ff), BF16),
        pltpu.VMEM((w4.shape[0] * mult, width), BF16),
        pltpu.VMEM((seq, seq), BF16),
        pltpu.VMEM((seq, width), F32),
        pltpu.VMEM((seq, width), BF16),
        pltpu.VMEM((seq, 3 * width), BF16),
        pltpu.VMEM((seq, width), BF16),
        pltpu.VMEM((seq, width), F32),
        pltpu.VMEM((seq, width), BF16),
        pltpu.VMEM((seq, ff), BF16),
        pltpu.VMEM((seq, ff), BF16),
        pltpu.VMEM((IMAGES * HEADS, seq // IMAGES, seq // IMAGES), BF16),
        pltpu.VMEM((seq, width), BF16),
        pltpu.VMEM((seq, width), F32),
        pltpu.VMEM((seq, width), BF16),
        pltpu.VMEM((5, seq, 1), F32),
        pltpu.VMEM((PROMPTS, width), F32),
        pltpu.VMEM((1, seq), jnp.int32),
        pltpu.VMEM((1, seq), jnp.int32),
        pltpu.VMEM((1, seq), jnp.int32),
        pltpu.VMEM((1, width), F32),
        pltpu.VMEM((1, width), F32),
        pltpu.VMEM((1, 3 * width), F32),
        pltpu.VMEM((1, width), F32),
        pltpu.VMEM((1, width), F32),
        pltpu.VMEM((1, width), F32),
        pltpu.VMEM((1, ff), F32),
        pltpu.VMEM((1, width), F32),
        pltpu.VMEM((acc_rows, width), F32),
        pltpu.VMEM((acc_rows // 2, width), F32),
        pltpu.VMEM((acc_rows // 2, width), F32),
        pltpu.VMEM((3, acc_rows // 8, width), F32),
        pltpu.VMEM((4, acc_rows // 8, width), F32),
        pltpu.VMEM((acc_rows, width), F32),
        dma((14,)),
        dma((4,)),
        dma((2, IMAGES)),
        dma((4, 31)),
        dma((4, 32)),
        dma((11,)),
        dma((11,)),
    ]
    any_spec = pl.BlockSpec(memory_space=pl.ANY)
    params = dict(vmem_limit_bytes=VMEM_LIMIT)
    if remote:
        params.update(collective_id=0, has_side_effects=True)
    return pl.pallas_call(
        functools.partial(kernel, remote, shards),
        out_shape=(
            jax.ShapeDtypeStruct(tokens.shape, BF16),
            jax.ShapeDtypeStruct(tokens.shape, BF16),
            jax.ShapeDtypeStruct((PROMPTS, width), F32),
        ),
        in_specs=[any_spec] * len(operands),
        out_specs=(any_spec, any_spec, pl.BlockSpec(memory_space=pltpu.VMEM)),
        scratch_shapes=scratch,
        compiler_params=pltpu.CompilerParams(**params),
    )(*operands)


def solution(mesh):
    devices = mesh.shape["dp"]

    def body(*args):
        weights = [args[i] for i in (7, 9, 13, 15)]
        shards = tuple(w.shape[0] for w in weights)
        if devices == 32 and all(n % 8 == 0 for n in shards):
            return layer(True, shards, args, weights)
        full = [lax.all_gather(w, "dp", axis=0, tiled=True) for w in weights]
        output, grad_tokens, grad_prompt = layer(False, shards, args, full)
        return output, grad_tokens, lax.psum(grad_prompt, "dp")

    rows = P("dp", None)
    cube = P("dp", None, None)
    in_specs = (
        cube, P(), rows, rows, rows, P(), P(), rows, P(), rows, P(), P(), P(), rows, P(), rows, P(), cube,
    )
    return jax.shard_map(body, mesh=mesh, in_specs=in_specs, out_specs=(cube, cube, P()), check_vma=False)
```

```python
import functools

import jax
import jax.numpy as jnp
from jax import lax
from jax.experimental import pallas as pl
from jax.experimental.pallas import tpu as pltpu
from jax.sharding import PartitionSpec as P

HEADS = 12
HEAD_DIM = 64
PROMPTS = 50
PATCHES = 196
IMAGES = 4
IMAGE_SLOTS = 1 + PROMPTS + PATCHES
PARTS = 3
EPS = 1e-06
BIG_NEGATIVE = -1e30
MESH = pl.DeviceIdType.MESH
F32 = jnp.float32
BF16 = jnp.bfloat16
DIMS = (4, 2, 2, 2)
VMEM_LIMIT = 67043328

def dot(a, b):
    return jnp.dot(a, b, preferred_element_type=F32)


def dot_t(a, b):
    return lax.dot_general(a, b, (((1,), (1,)), ((), ())), preferred_element_type=F32)


def t_dot(a, b):
    return lax.dot_general(a, b, (((0,), (0,)), ((), ())), preferred_element_type=F32)


def gelu_both(x):
    phi = 0.5 + 0.5 * lax.erf(x * 0.7071067811865476)
    density = jnp.exp2(x * (x * -0.7213475204444817))
    return x * phi, phi + x * (density * 0.3989422804014327)


class Gather:
    def __init__(self, srcs, dsts, rows, send_sem, recv_sem):
        Z, Y, X, C = DIMS
        self.src, self.dst, self.rows = srcs, dsts, rows
        self.send_sem, self.recv_sem = send_sem, recv_sem
        me = lax.axis_index("dp")
        self.me = me
        self.c = lax.rem(me, C)
        self.x = lax.rem(me // C, X)
        self.y = lax.rem(me // (C * X), Y)
        self.z = me // (C * X * Y)
        self.core = self.dev(self.z, self.y, self.x, 1 - self.c)
        self.xp = self.dev(self.z, self.y, 1 - self.x, self.c)
        self.yp = self.dev(self.z, 1 - self.y, self.x, self.c)
        self.dp = self.dev(self.z, 1 - self.y, 1 - self.x, self.c)
        self.zp = [self.dev(self.zo(j), self.y, self.x, self.c) for j in (1, 2, 3)]
        self.sent = [0] * len(rows)

    def dev(self, z, y, x, c):
        Z, Y, X, C = DIMS
        return ((z * Y + y) * X + x) * C + c

    def zo(self, j):
        return lax.rem(self.z + j, DIMS[0])

    def enter(self):
        barrier = pltpu.get_barrier_semaphore()
        peers = self.zp + [self.xp, self.yp, self.dp, self.core]
        for peer in peers:
            pl.semaphore_signal(barrier, inc=1, device_id=(peer,), device_id_type=MESH)
        pl.semaphore_wait(barrier, len(peers))

    def slot(self, k, owner):
        return self.dst[k].at[pl.ds(pl.multiple_of(owner * self.rows[k], 8), self.rows[k]), :]

    def copy(self, k, n, owner, to, src=None):
        slot = self.slot(k, owner)
        return pltpu.make_async_remote_copy(
            src_ref=slot if src is None else src,
            dst_ref=slot,
            send_sem=self.send_sem.at[k, n],
            recv_sem=self.recv_sem.at[k, owner],
            device_id=(to,),
            device_id_type=MESH,
        )

    def send(self, k, owner, to, src=None):
        self.copy(k, self.sent[k], owner, to, src).start()
        self.sent[k] += 1

    def wait(self, k, owner):
        self.copy(k, 0, owner, self.core).wait_recv()

    def line(self, k):
        for to in self.zp:
            self.send(k, self.me, to, self.src[k])

    def own(self, k):
        for to in (self.xp, self.yp, self.core):
            self.send(k, self.me, to, self.src[k])

    def column(self, k):
        for j in (1, 3, 2):
            owner = self.dev(self.zo(j), self.y, self.x, self.c)
            self.wait(k, owner)
            for to in (self.xp, self.yp, self.core):
                self.send(k, owner, to)

    def plane(self, k):
        for j in range(4):
            owner = self.dev(self.zo(j), self.y, 1 - self.x, self.c)
            self.wait(k, owner)
            if j < 2:
                self.send(k, owner, self.yp)
            self.send(k, owner, self.core)
            owner = self.dev(self.zo(j), 1 - self.y, self.x, self.c)
            self.wait(k, owner)
            if j >= 2:
                self.send(k, owner, self.xp)
            self.send(k, owner, self.core)

    def corner(self, k):
        for j in range(4):
            owner = self.dev(self.zo(j), 1 - self.y, 1 - self.x, self.c)
            self.wait(k, owner)
            self.send(k, owner, self.core)

    def arrive(self, k):
        @pl.loop(0, DIMS[0] * DIMS[1] * DIMS[2])
        def _(chip):
            self.wait(k, chip * DIMS[3] + 1 - self.c)

    def drain(self):
        for k, n in enumerate(self.sent):
            for i in range(n):
                self.copy(k, i, self.me, self.core).wait_send()


class Reduce:
    def __init__(self, g, acc, came, half, plane, line, total, sems):
        self.g, self.acc, self.came, self.half, self.plane, self.line, self.total = (
            g, acc, came, half, plane, line, total
        )
        self.send_sem, self.recv_sem = sems
        self.n = 0
        rows = acc.shape[0] // 8
        self.rows = rows
        self.mine = g.c * 4 + g.y * 2 + g.x

    def tile(self, ref, i):
        return ref.at[pl.ds(pl.multiple_of(i * self.rows, 8), self.rows), :]

    def exchange(self, moves):
        copies = []
        for src, dst, to in moves:
            copies.append(
                pltpu.make_async_remote_copy(
                    src_ref=src,
                    dst_ref=dst,
                    send_sem=self.send_sem.at[self.n],
                    recv_sem=self.recv_sem.at[self.n],
                    device_id=(to,),
                    device_id_type=MESH,
                )
            )
            self.n += 1
        for copy in copies:
            copy.start()
        return copies

    def steps(self):
        g, r = self.g, self.rows
        four = 4 * r

        def halves(ref, c):
            return ref.at[pl.ds(pl.multiple_of(c * four, 8), four), :]

        one = self.exchange([(halves(self.acc, 1 - g.c), self.came.at[:, :], g.core)])
        yield
        for copy in one:
            copy.wait()
        mine = pl.ds(pl.multiple_of(g.c * four, 8), four)
        self.half[:, :] = self.acc[mine, :] + self.came[:, :]
        moves = []
        for i, (dy, dx, to) in enumerate(((0, 1, g.xp), (1, 0, g.yp), (1, 1, g.dp))):
            y = g.y if dy == 0 else 1 - g.y
            x = g.x if dx == 0 else 1 - g.x
            moves.append((self.tile(self.half, y * 2 + x), self.plane.at[i], to))
        two = self.exchange(moves)
        yield
        for copy in two:
            copy.wait()
        own = pl.ds(pl.multiple_of((g.y * 2 + g.x) * r, 8), r)
        self.line[pl.ds(g.z, 1)] = (
            (self.half[own, :] + self.plane[0]) + (self.plane[1] + self.plane[2])
        )[None]
        three = self.exchange([(self.line.at[g.z], self.line.at[g.z], to) for to in g.zp])
        yield
        for copy in three:
            copy.wait()
        total = (self.line[0] + self.line[1]) + (self.line[2] + self.line[3])
        self.total[pl.ds(pl.multiple_of(self.mine * r, 8), r), :] = total
        mine_ref = self.tile(self.total, self.mine)
        four_c = self.exchange([(mine_ref, mine_ref, to) for to in (g.xp, g.yp, g.dp)])
        yield
        for copy in four_c:
            copy.wait()
        five = self.exchange([(halves(self.total, g.c), halves(self.total, g.c), g.core)])
        yield
        for copy in five:
            copy.wait()
        yield


def kernel(remote, shards, *refs):
    names = (
        "tokens", "prompt", "seg", "pads", "slots", "g1", "s1", "w1", "b1", "w2", "b2", "g2", "s2", "w3", "b3",
        "w4", "b4", "cot", "output", "grad_tokens", "grad_prompt", "W1a", "W1b", "W1c", "W2", "W3", "W4", "perm", "start",
        "first", "qkv", "mixed", "middle", "hidden", "slope", "probs", "gres", "gmid", "gmixed",
        "stats", "prompt_v", "seg_v", "pads_v", "slots_v", "g1_v", "s1_v", "b1_v", "b2_v", "g2_v", "s2_v",
        "b3_v", "b4_v", "acc", "came", "half", "plane", "line", "total", "in_sem", "loc_sem", "out_sem",
        "send_sem", "recv_sem", "rsend_sem", "rrecv_sem",
    )
    r = dict(zip(names, refs))
    seq, width = r["start"].shape
    block = seq // IMAGES
    pads_block = block - IMAGE_SLOTS
    ff = r["W3"].shape[1]
    pairs = HEADS // 2
    weights = [r["W1a"], r["W1b"], r["W1c"], r["W2"], r["W3"], r["W4"]]
    third = width // PARTS

    def rows_of(b):
        return pl.ds(pl.multiple_of(b * block, block), block)

    small = []
    for i, name in enumerate(
        ("slots", "seg", "pads", "prompt", "g1", "s1", "b1", "b2", "g2", "s2", "b3", "b4")
    ):
        small.append(pltpu.make_async_copy(r[name], r[name + "_v"], r["in_sem"].at[i]))
    tok_in = pltpu.make_async_copy(r["tokens"].at[0], r["gmixed"], r["in_sem"].at[12])
    cot_in = pltpu.make_async_copy(r["cot"].at[0], r["mixed"], r["in_sem"].at[13])
    for copy in small + [tok_in, cot_in]:
        copy.start()
    srcs = [None] * PARTS + [r["w2"], r["w3"], r["w4"]]
    g = Gather(srcs, weights, shards, r["send_sem"], r["recv_sem"]) if remote else None
    local = []
    for k, dst in enumerate(weights):
        if remote:
            dst = g.slot(k, g.me)
        if k >= PARTS:
            local.append([pltpu.make_async_copy(srcs[k], dst, r["loc_sem"].at[k, 0])])
            continue
        local.append(
            [
                pltpu.make_async_copy(
                    r["w1"].at[:, pl.ds(j * width + k * third, third)],
                    dst.at[:, pl.ds(j * third, third)],
                    r["loc_sem"].at[k, j],
                )
                for j in range(3)
            ]
        )
    for copies in local:
        for copy in copies:
            copy.start()

    def comm(*words):
        if remote:
            for word in words:
                getattr(g, word[:-1])(int(word[-1]))

    def at(i, table):
        for step, words in table.items() if remote else ():
            pl.when(i == step)(functools.partial(comm, *words))

    def have(k):
        if k >= PARTS:
            local[k][0].wait()
        if remote:
            g.arrive(k)

    if remote:
        g.enter()
    for k in range(PARTS):
        for copy in local[k]:
            copy.wait()
        if k == 0:
            comm("line0", "own0")
    comm("line1", "own1", "line2", "own2", "line3", "line4", "line5", "own3", "own4", "own5")

    for copy in small:
        copy.wait()
    seg = r["seg_v"][...]
    slots = r["slots_v"][...]
    is_prompt = slots < PROMPTS
    group = jnp.where(is_prompt, -1, seg)
    wanted = lax.broadcasted_iota(jnp.int32, (8, seq), 0)
    member = (wanted == group).astype(F32)
    lane = 128
    before = (
        lax.broadcasted_iota(jnp.int32, (lane, lane), 0) < lax.broadcasted_iota(jnp.int32, (lane, lane), 1)
    ).astype(F32).astype(BF16)
    counts = []
    offset = jnp.zeros((8, 1), F32)
    for i in range(seq // lane):
        part = member[:, i * lane : (i + 1) * lane]
        counts.append(dot(part.astype(BF16), before) + offset)
        offset = offset + jnp.sum(part, axis=1, keepdims=True)
    rank = jnp.sum(jnp.concatenate(counts, axis=1) * member, axis=0, keepdims=True).astype(jnp.int32)
    part_of = jnp.zeros_like(rank)
    for i in range(1, IMAGES):
        part_of = part_of + (rank >= i * pads_block).astype(jnp.int32)
    pad_dest = part_of * block + IMAGE_SLOTS + (rank - part_of * pads_block)
    image_dest = seg * block + jnp.where(is_prompt, slots, PROMPTS + rank)
    dest = jnp.where(seg < IMAGES, image_dest, pad_dest)
    live_dest = jnp.where(r["pads_v"][...] == 0, dest, -1)

    def norm_stats(v):
        mean = jnp.mean(v, axis=-1, keepdims=True)
        centered = v - mean
        return centered, lax.rsqrt(jnp.mean(centered * centered, axis=-1, keepdims=True) + EPS), mean

    tok_in.wait()
    cot_in.wait()
    head_rows = -(-PROMPTS // 8) * 8

    def place(b, carry):
        rows = rows_of(b)
        row_id = lax.broadcasted_iota(jnp.int32, (block, seq), 0) + b * block
        one_hot = (row_id == dest).astype(F32).astype(BF16)
        x = dot(one_hot, r["gmixed"][...])
        r["start"][rows, :] = x
        r["start"][pl.ds(pl.multiple_of(b * block, block), PROMPTS), :] = r["prompt_v"][...]
        centered, rstd, mean = norm_stats(r["start"][rows, :])
        r["stats"][0, rows, :] = mean
        r["stats"][1, rows, :] = rstd
        r["first"][rows, :] = (centered * rstd * r["g1_v"][...] + r["s1_v"][...]).astype(BF16)
        live = (row_id == live_dest).astype(F32).astype(BF16)
        r["gres"][rows, :] = dot(live, r["mixed"][...]).astype(BF16)
        return carry

    lax.fori_loop(0, IMAGES, place, 0)
    dest_col = jnp.transpose(jnp.broadcast_to(dest.astype(F32), (8, seq)))[:, 0:1].astype(jnp.int32)
    r["stats"][3, :, :] = dest_col.astype(F32)

    def inverse(b, carry):
        rows = rows_of(b)
        col = r["stats"][3, rows, :].astype(jnp.int32)
        r["perm"][rows, :] = (lax.broadcasted_iota(jnp.int32, (block, seq), 1) == col).astype(F32).astype(BF16)
        return carry

    lax.fori_loop(0, IMAGES, inverse, 0)

    scale = 1.0 / HEAD_DIM**0.5
    lanes = 2 * HEAD_DIM
    pairs_part = pairs // PARTS

    def pair_cols(p):
        return pl.ds(pl.multiple_of(p * lanes, lanes), lanes)

    def part_cols(j, p):
        part = p // pairs_part
        return pl.ds(pl.multiple_of(part * width + j * third + (p - part * pairs_part) * lanes, lanes), lanes)

    def project(t, b, carry):
        rows = rows_of(b)
        y = dot(r["first"][rows, :], weights[t][...])
        for j in range(3):
            bias = r["b1_v"][:, j * width + t * third : j * width + (t + 1) * third]
            part = (y[:, j * third : (j + 1) * third] + bias).astype(BF16)
            r["qkv"][rows, t * width + j * third : t * width + (j + 1) * third] = part * scale if j == 0 else part
        return carry

    def lanes_of(h):
        low = lax.broadcasted_iota(jnp.int32, (1, lanes), 1) < HEAD_DIM
        return (low if h == 0 else jnp.logical_not(low)).astype(F32).astype(BF16)

    def attention(load, groups, bias):
        scores, probs, outs = [], [], []
        for u in range(groups):
            q, k = load(u, 0), load(u, 1)
            scores += [dot_t(q * lanes_of(h), k) + bias for h in range(2)]
        for s in scores:
            e = jnp.exp(s - jnp.max(s, axis=-1, keepdims=True))
            probs.append((e * (1.0 / jnp.sum(e, axis=-1, keepdims=True))).astype(BF16))
        for u in range(groups):
            v = load(u, 2)
            out = dot(probs[2 * u], v * lanes_of(0)) + dot(probs[2 * u + 1], v * lanes_of(1))
            outs.append(out.astype(BF16))
        return probs, outs

    def bias_of(shape, bad):
        return jnp.where(bad(lax.broadcasted_iota(jnp.int32, shape, 1)), BIG_NEGATIVE, 0.0)

    at_once = 4

    def pair_of(t, i):
        return i // pairs_part, t * pairs_part + lax.rem(i, pairs_part)

    def attend(t, table, i, carry):
        at(i, table)
        where = [pair_of(t, i * at_once + u) for u in range(at_once)]

        def load(u, j):
            b, p = where[u]
            return r["qkv"][rows_of(b), part_cols(j, p)]

        probs, outs = attention(load, at_once, bias_of((1, block), lambda col: col >= IMAGE_SLOTS))
        for u, (b, p) in enumerate(where):
            for h in range(2):
                r["probs"][2 * (b * pairs + p) + h] = probs[2 * u + h]
            r["mixed"][rows_of(b), pair_cols(p)] = outs[u]
        return carry

    tables = (
        {0: ("plane2",), 1: ("corner1",)},
        {0: ("column4",), 1: ("plane3", "corner2")},
        {1: ("corner3",)},
    )
    comm("column0", "column1", "plane0", "column2", "plane1", "corner0", "column3")
    for t in range(PARTS):
        have(t)
        lax.fori_loop(0, IMAGES, functools.partial(project, t), 0)
        lax.fori_loop(0, IMAGES * pairs_part // at_once, functools.partial(attend, t, tables[t]), 0)

    tail = 16
    group_rows = IMAGES * tail

    def attend_pads(p, carry):
        def load(u, j):
            return jnp.concatenate(
                [
                    r["qkv"][b * block + block - tail : (b + 1) * block, part_cols(j, 2 * p + u)]
                    for b in range(IMAGES)
                ],
                axis=0,
            )

        bias = bias_of((1, group_rows), lambda col: lax.rem(col, tail) < tail - pads_block)
        outs = attention(load, 2, bias)[1]
        is_pad = lax.broadcasted_iota(jnp.int32, (tail, lanes), 0) >= tail - pads_block
        for u in range(2):
            for b in range(IMAGES):
                where = slice(b * block + block - tail, (b + 1) * block)
                old = r["mixed"][where, pair_cols(2 * p + u)]
                r["mixed"][where, pair_cols(2 * p + u)] = jnp.where(is_pad, outs[u][b * tail : (b + 1) * tail], old)
        return carry

    lax.fori_loop(0, pairs // 2, attend_pads, 0)
    have(3)

    def two(i):
        return [rows_of(2 * i), rows_of(2 * i + 1)]

    def join(i, carry):
        terms = [dot(r["mixed"][rows, :], r["W2"][...]) for rows in two(i)]
        for rows, term in zip(two(i), terms):
            middle = r["start"][rows, :] + (term + r["b2_v"][...])
            r["middle"][rows, :] = middle
            centered, rstd, mean = norm_stats(middle)
            r["stats"][2, rows, :] = mean
            r["stats"][3, rows, :] = rstd
            r["first"][rows, :] = (centered * rstd * r["g2_v"][...] + r["s2_v"][...]).astype(BF16)
        return carry

    lax.fori_loop(0, IMAGES // 2, join, 0)
    comm("column5", "plane4", "corner4")
    have(4)
    parts = ff // width

    def expand(i, carry):
        b, n = i // parts, lax.rem(i, parts)
        at(i, {2: ("plane5",), 8: ("corner5",)})
        rows = rows_of(b)
        cols = pl.ds(pl.multiple_of(n * width, width), width)
        pre = dot(r["first"][rows, :], r["W3"][:, cols]) + r["b3_v"][:, cols]
        hidden, slope = gelu_both(pre)
        r["hidden"][rows, cols] = hidden.astype(BF16)
        r["slope"][rows, cols] = slope.astype(BF16)
        return carry

    lax.fori_loop(0, IMAGES * parts, expand, 0)
    have(5)

    def back_hidden(i, carry):
        b, n = i // parts, lax.rem(i, parts)
        rows = rows_of(b)
        cols = pl.ds(pl.multiple_of(n * width, width), width)
        grad = dot_t(r["gres"][rows, :], r["W4"][cols, :])
        r["slope"][rows, cols] = (grad * r["slope"][rows, cols].astype(F32)).astype(BF16)
        return carry

    lax.fori_loop(0, IMAGES * parts, back_hidden, 0)

    def norm_back(grad, v, mean, rstd, gain):
        unit = (v - mean) * rstd
        scaled = grad * gain
        first = jnp.mean(scaled, axis=-1, keepdims=True)
        second = jnp.mean(scaled * unit, axis=-1, keepdims=True)
        return rstd * (scaled - first - unit * second)

    def back_join(i, carry):
        terms = [dot_t(r["slope"][rows, :], r["W3"][...]) for rows in two(i)]
        grads = []
        for rows, term in zip(two(i), terms):
            grad = norm_back(
                term, r["middle"][rows, :], r["stats"][2, rows, :], r["stats"][3, rows, :], r["g2_v"][...]
            )
            grad = r["gres"][rows, :].astype(F32) + grad
            r["gmid"][rows, :] = grad
            grads.append(grad.astype(BF16))
        for rows, grad in zip(two(i), grads):
            r["gmixed"][rows, :] = dot_t(grad, r["W2"][...]).astype(BF16)
        return carry

    lax.fori_loop(0, IMAGES // 2, back_join, 0)

    back_once = 3

    def back_attend(i, carry):
        where = [((i * back_once + u) // pairs, lax.rem(i * back_once + u, pairs)) for u in range(back_once)]

        def load(u, j):
            b, p = where[u]
            return r["qkv"][rows_of(b), part_cols(j, p)]

        def store(u, j, value):
            b, p = where[u]
            r["qkv"][rows_of(b), part_cols(j, p)] = value

        heads = [(u, h) for u in range(back_once) for h in range(2)]
        queries, keys, grads, shifted = [], [], [], []
        for u, (b, p) in enumerate(where):
            queries.append(load(u, 0))
            keys.append(load(u, 1))
            v = load(u, 2)
            go = r["gmixed"][rows_of(b), pair_cols(p)]
            inner = go.astype(F32) * r["mixed"][rows_of(b), pair_cols(p)].astype(F32)
            inner = pltpu.roll(inner, HEAD_DIM, 1).astype(BF16)
            grads.append(go)
            for h in range(2):
                own, other = lanes_of(h), lanes_of(1 - h)
                shifted.append(dot_t(go * own + inner * other, v * own - other))
        grads_t = [jnp.transpose(x) for x in grads]
        queries_t = [jnp.transpose(x) for x in queries]
        probs = [r["probs"][2 * (b * pairs + p) + h] for b, p in where for h in range(2)]
        half = [slice(0, HEAD_DIM), slice(HEAD_DIM, lanes)]
        grad_v = [dot(grads_t[u][half[h]], probs[2 * u + h]) for u, h in heads]
        ds = [(probs[n].astype(F32) * shifted[n]).astype(BF16) for n in range(len(heads))]
        for u in range(back_once):
            grad_q = dot(ds[2 * u], keys[u] * lanes_of(0)) + dot(ds[2 * u + 1], keys[u] * lanes_of(1))
            store(u, 0, (grad_q * scale).astype(BF16))
        for u in range(back_once):
            grad_k = [dot(queries_t[u][half[h]], ds[2 * u + h]) for h in range(2)]
            store(u, 1, jnp.transpose(jnp.concatenate(grad_k, axis=0).astype(BF16)))
            store(u, 2, jnp.transpose(jnp.concatenate(grad_v[2 * u : 2 * u + 2], axis=0).astype(BF16)))
        return carry

    lax.fori_loop(0, IMAGES * pairs // back_once, back_attend, 0)

    r["acc"][...] = jnp.zeros_like(r["acc"])
    heads_at = lax.broadcasted_iota(jnp.int32, (block, width), 0)

    def back_start(i, carry):
        terms = []
        for rows in two(i):
            grad = dot_t(r["qkv"][rows, 0:width], weights[0][...])
            for t in range(1, PARTS):
                grad = grad + dot_t(r["qkv"][rows, t * width : (t + 1) * width], weights[t][...])
            terms.append(grad)
        keep = lax.broadcasted_iota(jnp.int32, (head_rows, width), 0) < PROMPTS
        for rows, term in zip(two(i), terms):
            grad = norm_back(
                term, r["start"][rows, :], r["stats"][0, rows, :], r["stats"][1, rows, :], r["g1_v"][...]
            )
            grad = r["gmid"][rows, :] + grad
            top = grad[0:head_rows, :]
            r["acc"][0:head_rows, :] = r["acc"][0:head_rows, :] + jnp.where(keep, top, 0.0)
            r["first"][rows, :] = jnp.where(heads_at < PROMPTS, 0.0, grad).astype(BF16)
        return carry

    lax.fori_loop(0, IMAGES // 2, back_start, 0)

    if remote:
        red = Reduce(
            g, *(r[name] for name in ("acc", "came", "half", "plane", "line", "total")), (r["rsend_sem"], r["rrecv_sem"])
        ).steps()
    else:
        r["total"][...] = r["acc"][...]
        red = iter(range(6))
    next(red)

    def reduce_out(b):
        rows = rows_of(b)
        y = r["middle"][rows, :] + (dot(r["hidden"][rows, :], r["W4"][...]) + r["b4_v"][...])
        r["gres"][rows, :] = y.astype(BF16)

    def ship(b, src, stage, out, n):
        rows = rows_of(b)
        r[stage][rows, :] = dot(r["perm"][rows, :], r[src][...]).astype(BF16)
        pltpu.make_async_copy(r[stage].at[rows, :], r[out].at[0, rows, :], r["out_sem"].at[n, b]).start()

    def tokens_out(*blocks):
        for b in blocks:
            ship(b, "first", "gmixed", "grad_tokens", 0)

    def rows_out(*blocks):
        for b in blocks:
            ship(b, "gres", "mixed", "output", 1)

    tokens_out(0, 1)
    next(red)
    reduce_out(0)
    tokens_out(2, 3)
    next(red)
    for b in range(1, IMAGES):
        reduce_out(b)
    next(red)
    rows_out(0, 1, 2)
    next(red)
    rows_out(3)
    next(red)
    r["grad_prompt"][...] = r["total"][0:PROMPTS, :]
    for n, (stage, out) in enumerate((("gmixed", "grad_tokens"), ("mixed", "output"))):
        for b in range(IMAGES):
            rows = slice(b * block, (b + 1) * block)
            pltpu.make_async_copy(r[stage].at[rows, :], r[out].at[0, rows, :], r["out_sem"].at[n, b]).wait()
    if remote:
        g.drain()


def layer(remote, shards, args, full):
    (tokens, prompt, seg, pads, slots, g1, s1, _, b1, _, b2, g2, s2, _, b3, _, b4, cot) = args
    w1, w2, w3, w4 = full
    _, seq, width = tokens.shape
    ff = b3.shape[0]
    mult = 32 if remote else 1
    row = lambda v: v.reshape(1, -1)
    operands = [
        tokens, prompt, seg, pads, slots, row(g1), row(s1), w1, row(b1), w2, row(b2), row(g2), row(s2),
        w3, row(b3), w4, row(b4), cot,
    ]
    acc_rows = 64
    dma = pltpu.SemaphoreType.DMA
    scratch = [
        *[pltpu.VMEM((w1.shape[0] * mult, 3 * width // PARTS), BF16)] * PARTS,
        pltpu.VMEM((w2.shape[0] * mult, width), BF16),
        pltpu.VMEM((w3.shape[0] * mult, ff), BF16),
        pltpu.VMEM((w4.shape[0] * mult, width), BF16),
        pltpu.VMEM((seq, seq), BF16),
        pltpu.VMEM((seq, width), F32),
        pltpu.VMEM((seq, width), BF16),
        pltpu.VMEM((seq, 3 * width), BF16),
        pltpu.VMEM((seq, width), BF16),
        pltpu.VMEM((seq, width), F32),
        pltpu.VMEM((seq, ff), BF16),
        pltpu.VMEM((seq, ff), BF16),
        pltpu.VMEM((IMAGES * HEADS, seq // IMAGES, seq // IMAGES), BF16),
        pltpu.VMEM((seq, width), BF16),
        pltpu.VMEM((seq, width), F32),
        pltpu.VMEM((seq, width), BF16),
        pltpu.VMEM((4, seq, 1), F32),
        pltpu.VMEM((PROMPTS, width), F32),
        pltpu.VMEM((1, seq), jnp.int32),
        pltpu.VMEM((1, seq), jnp.int32),
        pltpu.VMEM((1, seq), jnp.int32),
        pltpu.VMEM((1, width), F32),
        pltpu.VMEM((1, width), F32),
        pltpu.VMEM((1, 3 * width), F32),
        pltpu.VMEM((1, width), F32),
        pltpu.VMEM((1, width), F32),
        pltpu.VMEM((1, width), F32),
        pltpu.VMEM((1, ff), F32),
        pltpu.VMEM((1, width), F32),
        pltpu.VMEM((acc_rows, width), F32),
        pltpu.VMEM((acc_rows // 2, width), F32),
        pltpu.VMEM((acc_rows // 2, width), F32),
        pltpu.VMEM((3, acc_rows // 8, width), F32),
        pltpu.VMEM((4, acc_rows // 8, width), F32),
        pltpu.VMEM((acc_rows, width), F32),
        dma((14,)),
        dma((PARTS + 3, 3)),
        dma((2, IMAGES)),
        dma((PARTS + 3, 31)),
        dma((PARTS + 3, 32)),
        dma((11,)),
        dma((11,)),
    ]
    any_spec = pl.BlockSpec(memory_space=pl.ANY)
    params = dict(vmem_limit_bytes=VMEM_LIMIT)
    if remote:
        params.update(collective_id=0, has_side_effects=True)
    return pl.pallas_call(
        functools.partial(kernel, remote, shards),
        out_shape=(
            jax.ShapeDtypeStruct(tokens.shape, BF16),
            jax.ShapeDtypeStruct(tokens.shape, BF16),
            jax.ShapeDtypeStruct((PROMPTS, width), F32),
        ),
        in_specs=[any_spec] * len(operands),
        out_specs=(any_spec, any_spec, pl.BlockSpec(memory_space=pltpu.VMEM)),
        scratch_shapes=scratch,
        compiler_params=pltpu.CompilerParams(**params),
    )(*operands)


def solution(mesh):
    devices = mesh.shape["dp"]

    def body(*args):
        weights = [args[i] for i in (7, 9, 13, 15)]
        shards = (weights[0].shape[0],) * PARTS + tuple(w.shape[0] for w in weights[1:])
        if devices == 32 and all(n % 8 == 0 for n in shards):
            return layer(True, shards, args, weights)
        full = [lax.all_gather(w, "dp", axis=0, tiled=True) for w in weights]
        output, grad_tokens, grad_prompt = layer(False, shards, args, full)
        return output, grad_tokens, lax.psum(grad_prompt, "dp")

    rows = P("dp", None)
    cube = P("dp", None, None)
    in_specs = (
        cube, P(), rows, rows, rows, P(), P(), rows, P(), rows, P(), P(), P(), rows, P(), rows, P(), cube,
    )
    return jax.shard_map(body, mesh=mesh, in_specs=in_specs, out_specs=(cube, cube, P()), check_vma=False)
```

```python
import functools

import jax
import jax.numpy as jnp
from jax import lax
from jax.experimental import pallas as pl
from jax.experimental.pallas import tpu as pltpu
from jax.sharding import PartitionSpec as P

HEADS = 12
HEAD_DIM = 64
PROMPTS = 50
PATCHES = 196
IMAGES = 4
IMAGE_SLOTS = 1 + PROMPTS + PATCHES
PARTS = 3
EPS = 1e-06
BIG_NEGATIVE = -1e30
MESH = pl.DeviceIdType.MESH
F32 = jnp.float32
BF16 = jnp.bfloat16
DIMS = (4, 2, 2, 2)
VMEM_LIMIT = 67043328

def dot(a, b):
    return jnp.dot(a, b, preferred_element_type=F32)


def dot_t(a, b):
    return lax.dot_general(a, b, (((1,), (1,)), ((), ())), preferred_element_type=F32)


def t_dot(a, b):
    return lax.dot_general(a, b, (((0,), (0,)), ((), ())), preferred_element_type=F32)


def gelu_both(x):
    phi = 0.5 + 0.5 * lax.erf(x * 0.7071067811865476)
    density = jnp.exp2(x * (x * -0.7213475204444817))
    return x * phi, phi + x * (density * 0.3989422804014327)


class Gather:
    def __init__(self, srcs, dsts, rows, send_sem, recv_sem):
        Z, Y, X, C = DIMS
        self.src, self.dst, self.rows = srcs, dsts, rows
        self.send_sem, self.recv_sem = send_sem, recv_sem
        me = lax.axis_index("dp")
        self.me = me
        self.c = lax.rem(me, C)
        self.x = lax.rem(me // C, X)
        self.y = lax.rem(me // (C * X), Y)
        self.z = me // (C * X * Y)
        self.core = self.dev(self.z, self.y, self.x, 1 - self.c)
        self.xp = self.dev(self.z, self.y, 1 - self.x, self.c)
        self.yp = self.dev(self.z, 1 - self.y, self.x, self.c)
        self.dp = self.dev(self.z, 1 - self.y, 1 - self.x, self.c)
        self.zp = [self.dev(self.zo(j), self.y, self.x, self.c) for j in (1, 2, 3)]
        self.sent = [0] * len(rows)

    def dev(self, z, y, x, c):
        Z, Y, X, C = DIMS
        return ((z * Y + y) * X + x) * C + c

    def zo(self, j):
        return lax.rem(self.z + j, DIMS[0])

    def enter(self):
        barrier = pltpu.get_barrier_semaphore()
        peers = self.zp + [self.xp, self.yp, self.dp, self.core]
        for peer in peers:
            pl.semaphore_signal(barrier, inc=1, device_id=(peer,), device_id_type=MESH)
        pl.semaphore_wait(barrier, len(peers))

    def slot(self, k, owner):
        return self.dst[k].at[pl.ds(pl.multiple_of(owner * self.rows[k], 8), self.rows[k]), :]

    def copy(self, k, n, owner, to, src=None):
        slot = self.slot(k, owner)
        return pltpu.make_async_remote_copy(
            src_ref=slot if src is None else src,
            dst_ref=slot,
            send_sem=self.send_sem.at[k, n],
            recv_sem=self.recv_sem.at[k, owner],
            device_id=(to,),
            device_id_type=MESH,
        )

    def send(self, k, owner, to, src=None):
        self.copy(k, self.sent[k], owner, to, src).start()
        self.sent[k] += 1

    def wait(self, k, owner):
        self.copy(k, 0, owner, self.core).wait_recv()

    def line(self, k):
        for to in self.zp:
            self.send(k, self.me, to, self.src[k])

    def own(self, k):
        for to in (self.xp, self.yp, self.core):
            self.send(k, self.me, to, self.src[k])

    def column(self, k, steps=(0, 1, 2)):
        for i in steps:
            owner = self.dev(self.zo((1, 3, 2)[i]), self.y, self.x, self.c)
            self.wait(k, owner)
            for to in (self.xp, self.yp, self.core):
                self.send(k, owner, to)

    def plane(self, k, steps=(0, 1, 2, 3)):
        for i in steps:
            j = (0, 1, 3, 2)[i]
            owner = self.dev(self.zo(j), self.y, 1 - self.x, self.c)
            self.wait(k, owner)
            if i < 2:
                self.send(k, owner, self.yp)
            self.send(k, owner, self.core)
            owner = self.dev(self.zo(j), 1 - self.y, self.x, self.c)
            self.wait(k, owner)
            if i >= 2:
                self.send(k, owner, self.xp)
            self.send(k, owner, self.core)

    def corner(self, k, steps=(0, 1, 2, 3)):
        for i in steps:
            owner = self.dev(self.zo((0, 1, 3, 2)[i]), 1 - self.y, 1 - self.x, self.c)
            self.wait(k, owner)
            self.send(k, owner, self.core)

    def arrive(self, k):
        @pl.loop(0, DIMS[0] * DIMS[1] * DIMS[2])
        def _(chip):
            self.wait(k, chip * DIMS[3] + 1 - self.c)

    def drain(self):
        for k, n in enumerate(self.sent):
            for i in range(n):
                self.copy(k, i, self.me, self.core).wait_send()


class Reduce:
    def __init__(self, g, acc, came, half, plane, line, total, sems):
        self.g, self.acc, self.came, self.half, self.plane, self.line, self.total = (
            g, acc, came, half, plane, line, total
        )
        self.send_sem, self.recv_sem = sems
        self.n = 0
        rows = acc.shape[0] // 8
        self.rows = rows
        self.mine = g.c * 4 + g.y * 2 + g.x

    def tile(self, ref, i):
        return ref.at[pl.ds(pl.multiple_of(i * self.rows, 8), self.rows), :]

    def exchange(self, moves):
        copies = []
        for src, dst, to in moves:
            copies.append(
                pltpu.make_async_remote_copy(
                    src_ref=src,
                    dst_ref=dst,
                    send_sem=self.send_sem.at[self.n],
                    recv_sem=self.recv_sem.at[self.n],
                    device_id=(to,),
                    device_id_type=MESH,
                )
            )
            self.n += 1
        for copy in copies:
            copy.start()
        return copies

    def steps(self):
        g, r = self.g, self.rows
        four = 4 * r

        def halves(ref, c):
            return ref.at[pl.ds(pl.multiple_of(c * four, 8), four), :]

        one = self.exchange([(halves(self.acc, 1 - g.c), self.came.at[:, :], g.core)])
        yield
        for copy in one:
            copy.wait()
        mine = pl.ds(pl.multiple_of(g.c * four, 8), four)
        self.half[:, :] = self.acc[mine, :] + self.came[:, :]
        moves = []
        for i, (dy, dx, to) in enumerate(((0, 1, g.xp), (1, 0, g.yp), (1, 1, g.dp))):
            y = g.y if dy == 0 else 1 - g.y
            x = g.x if dx == 0 else 1 - g.x
            moves.append((self.tile(self.half, y * 2 + x), self.plane.at[i], to))
        two = self.exchange(moves)
        yield
        for copy in two:
            copy.wait()
        own = pl.ds(pl.multiple_of((g.y * 2 + g.x) * r, 8), r)
        self.line[pl.ds(g.z, 1)] = (
            (self.half[own, :] + self.plane[0]) + (self.plane[1] + self.plane[2])
        )[None]
        three = self.exchange([(self.line.at[g.z], self.line.at[g.z], to) for to in g.zp])
        yield
        for copy in three:
            copy.wait()
        total = (self.line[0] + self.line[1]) + (self.line[2] + self.line[3])
        self.total[pl.ds(pl.multiple_of(self.mine * r, 8), r), :] = total
        mine_ref = self.tile(self.total, self.mine)
        four_c = self.exchange([(mine_ref, mine_ref, to) for to in (g.xp, g.yp, g.dp)])
        yield
        for copy in four_c:
            copy.wait()
        five = self.exchange([(halves(self.total, g.c), halves(self.total, g.c), g.core)])
        yield
        for copy in five:
            copy.wait()
        yield


def kernel(remote, shards, *refs):
    names = (
        "tokens", "prompt", "seg", "pads", "slots", "g1", "s1", "w1", "b1", "w2", "b2", "g2", "s2", "w3", "b3",
        "w4", "b4", "cot", "output", "grad_tokens", "grad_prompt", "W1a", "W1b", "W1c", "W2", "W3", "W4", "perm", "start",
        "first", "qkv", "mixed", "middle", "hidden", "slope", "probs", "gres", "gmid", "gmixed",
        "stats", "prompt_v", "seg_v", "pads_v", "slots_v", "g1_v", "s1_v", "b1_v", "b2_v", "g2_v", "s2_v",
        "b3_v", "b4_v", "acc", "came", "half", "plane", "line", "total", "in_sem", "loc_sem", "out_sem",
        "send_sem", "recv_sem", "rsend_sem", "rrecv_sem",
    )
    r = dict(zip(names, refs))
    seq, width = r["start"].shape
    block = seq // IMAGES
    pads_block = block - IMAGE_SLOTS
    ff = r["W3"].shape[1]
    pairs = HEADS // 2
    weights = [r["W1a"], r["W1b"], r["W1c"], r["W2"], r["W3"], r["W4"]]
    third = width // PARTS

    def rows_of(b):
        return pl.ds(pl.multiple_of(b * block, block), block)

    small = []
    for i, name in enumerate(
        ("slots", "seg", "pads", "prompt", "g1", "s1", "b1", "b2", "g2", "s2", "b3", "b4")
    ):
        dst = r[name + "_v"]
        small.append(pltpu.make_async_copy(r[name], dst if i < 4 else dst.at[0], r["in_sem"].at[i]))
    tok_in = pltpu.make_async_copy(r["tokens"].at[0], r["gmixed"], r["in_sem"].at[12])
    cot_in = pltpu.make_async_copy(r["cot"].at[0], r["mixed"], r["in_sem"].at[13])
    for copy in small + [tok_in, cot_in]:
        copy.start()
    srcs = [None] * PARTS + [r["w2"], r["w3"], r["w4"]]
    g = Gather(srcs, weights, shards, r["send_sem"], r["recv_sem"]) if remote else None
    local = []
    for k, dst in enumerate(weights):
        if remote:
            dst = g.slot(k, g.me)
        if k >= PARTS:
            local.append([pltpu.make_async_copy(srcs[k], dst, r["loc_sem"].at[k, 0])])
            continue
        local.append(
            [
                pltpu.make_async_copy(
                    r["w1"].at[:, pl.ds(j * width + k * third, third)],
                    dst.at[:, pl.ds(j * third, third)],
                    r["loc_sem"].at[k, j],
                )
                for j in range(3)
            ]
        )
    for copies in local:
        for copy in copies:
            copy.start()

    def comm(*words):
        if remote:
            for word in words:
                word, _, steps = word.partition(":")
                step = getattr(g, word[:-1])
                step(int(word[-1]), *([tuple(int(i) for i in steps)] if steps else []))

    def at(i, table):
        for step, words in table.items() if remote else ():
            pl.when(i == step)(functools.partial(comm, *words))

    def have(k):
        if k >= PARTS:
            local[k][0].wait()
        if remote:
            g.arrive(k)

    if remote:
        g.enter()
    for k in range(PARTS):
        for copy in local[k]:
            copy.wait()
        if k == 0:
            comm("line0", "own0")
    comm("line1", "own1", "line2", "own2", "line3", "line4", "line5", "own3", "own4", "own5")

    for copy in small:
        copy.wait()
    seg = r["seg_v"][...]
    slots = r["slots_v"][...]
    is_prompt = slots < PROMPTS
    group = jnp.where(is_prompt, -1, seg)
    wanted = lax.broadcasted_iota(jnp.int32, (8, seq), 0)
    member = (wanted == group).astype(F32)
    lane = 128
    before = (
        lax.broadcasted_iota(jnp.int32, (lane, lane), 0) < lax.broadcasted_iota(jnp.int32, (lane, lane), 1)
    ).astype(F32).astype(BF16)
    counts = []
    offset = jnp.zeros((8, 1), F32)
    for i in range(seq // lane):
        part = member[:, i * lane : (i + 1) * lane]
        counts.append(dot(part.astype(BF16), before) + offset)
        offset = offset + jnp.sum(part, axis=1, keepdims=True)
    rank = jnp.sum(jnp.concatenate(counts, axis=1) * member, axis=0, keepdims=True).astype(jnp.int32)
    part_of = jnp.zeros_like(rank)
    for i in range(1, IMAGES):
        part_of = part_of + (rank >= i * pads_block).astype(jnp.int32)
    pad_dest = part_of * block + IMAGE_SLOTS + (rank - part_of * pads_block)
    image_dest = seg * block + jnp.where(is_prompt, slots, PROMPTS + rank)
    dest = jnp.where(seg < IMAGES, image_dest, pad_dest)
    live_dest = jnp.where(r["pads_v"][...] == 0, dest, -1)

    def norm_stats(v):
        mean = jnp.mean(v, axis=-1, keepdims=True)
        centered = v - mean
        return centered, lax.rsqrt(jnp.mean(centered * centered, axis=-1, keepdims=True) + EPS), mean

    tok_in.wait()
    cot_in.wait()
    head_rows = -(-PROMPTS // 8) * 8

    def place(b, carry):
        rows = rows_of(b)
        row_id = lax.broadcasted_iota(jnp.int32, (block, seq), 0) + b * block
        one_hot = (row_id == dest).astype(F32).astype(BF16)
        x = dot(one_hot, r["gmixed"][...])
        r["start"][rows, :] = x
        r["start"][pl.ds(pl.multiple_of(b * block, block), PROMPTS), :] = r["prompt_v"][...]
        centered, rstd, mean = norm_stats(r["start"][rows, :])
        r["stats"][0, rows, :] = mean
        r["stats"][1, rows, :] = rstd
        r["first"][rows, :] = (centered * rstd * r["g1_v"][...] + r["s1_v"][...]).astype(BF16)
        live = (row_id == live_dest).astype(F32).astype(BF16)
        r["gres"][rows, :] = dot(live, r["mixed"][...]).astype(BF16)
        return carry

    lax.fori_loop(0, IMAGES, place, 0)
    dest_col = jnp.transpose(jnp.broadcast_to(dest.astype(F32), (8, seq)))[:, 0:1].astype(jnp.int32)
    r["stats"][3, :, :] = dest_col.astype(F32)

    def inverse(b, carry):
        rows = rows_of(b)
        col = r["stats"][3, rows, :].astype(jnp.int32)
        r["perm"][rows, :] = (lax.broadcasted_iota(jnp.int32, (block, seq), 1) == col).astype(F32).astype(BF16)
        return carry

    lax.fori_loop(0, IMAGES, inverse, 0)

    scale = 1.0 / HEAD_DIM**0.5
    lanes = 2 * HEAD_DIM
    pairs_part = pairs // PARTS

    def pair_cols(p):
        return pl.ds(pl.multiple_of(p * lanes, lanes), lanes)

    def part_cols(j, p):
        part = p // pairs_part
        return pl.ds(pl.multiple_of(part * width + j * third + (p - part * pairs_part) * lanes, lanes), lanes)

    def project(t, table, b, carry):
        at(b, table)
        rows = rows_of(b)
        y = dot(r["first"][rows, :], weights[t][...])
        for j in range(3):
            bias = r["b1_v"][:, j * width + t * third : j * width + (t + 1) * third]
            part = (y[:, j * third : (j + 1) * third] + bias).astype(BF16)
            r["qkv"][rows, t * width + j * third : t * width + (j + 1) * third] = part * scale if j == 0 else part
        return carry

    def lanes_of(h):
        low = lax.broadcasted_iota(jnp.int32, (1, lanes), 1) < HEAD_DIM
        return (low if h == 0 else jnp.logical_not(low)).astype(F32).astype(BF16)

    def attention(load, groups, bias):
        scores, probs, outs = [], [], []
        for u in range(groups):
            q, k = load(u, 0), load(u, 1)
            scores += [dot_t(q * lanes_of(h), k) + bias for h in range(2)]
        for s in scores:
            e = jnp.exp(s - jnp.max(s, axis=-1, keepdims=True))
            probs.append((e * (1.0 / jnp.sum(e, axis=-1, keepdims=True))).astype(BF16))
        for u in range(groups):
            v = load(u, 2)
            out = dot(probs[2 * u], v * lanes_of(0)) + dot(probs[2 * u + 1], v * lanes_of(1))
            outs.append(out.astype(BF16))
        return probs, outs

    def bias_of(shape, bad):
        return jnp.where(bad(lax.broadcasted_iota(jnp.int32, shape, 1)), BIG_NEGATIVE, 0.0)

    at_once = 4

    def pair_of(t, i):
        return i // pairs_part, t * pairs_part + lax.rem(i, pairs_part)

    def attend(t, table, i, carry):
        at(i, table)
        where = [pair_of(t, i * at_once + u) for u in range(at_once)]

        def load(u, j):
            b, p = where[u]
            return r["qkv"][rows_of(b), part_cols(j, p)]

        probs, outs = attention(load, at_once, bias_of((1, block), lambda col: col >= IMAGE_SLOTS))
        for u, (b, p) in enumerate(where):
            for h in range(2):
                r["probs"][2 * (b * pairs + p) + h] = probs[2 * u + h]
            r["mixed"][rows_of(b), pair_cols(p)] = outs[u]
        return carry

    tables = (
        ({1: ("plane2:01",), 3: ("plane2:23",)}, {0: ("corner1",), 1: ("plane3:01",)}),
        ({1: ("plane3:23",), 3: ("column4:0",)}, {0: ("corner2",), 1: ("column4:1",)}),
        ({1: ("column4:2",), 3: ("corner3",)}, {0: ("plane4:0",), 1: ("plane4:1",)}),
    )
    comm("column0", "column1", "plane0", "column2", "plane1", "column3", "corner0")
    for t in range(PARTS):
        have(t)
        lax.fori_loop(0, IMAGES, functools.partial(project, t, tables[t][0]), 0)
        lax.fori_loop(0, IMAGES * pairs_part // at_once, functools.partial(attend, t, tables[t][1]), 0)

    tail = 16
    group_rows = IMAGES * tail

    def attend_pads(p, carry):
        def load(u, j):
            return jnp.concatenate(
                [
                    r["qkv"][b * block + block - tail : (b + 1) * block, part_cols(j, 2 * p + u)]
                    for b in range(IMAGES)
                ],
                axis=0,
            )

        bias = bias_of((1, group_rows), lambda col: lax.rem(col, tail) < tail - pads_block)
        outs = attention(load, 2, bias)[1]
        is_pad = lax.broadcasted_iota(jnp.int32, (tail, lanes), 0) >= tail - pads_block
        for u in range(2):
            for b in range(IMAGES):
                where = slice(b * block + block - tail, (b + 1) * block)
                old = r["mixed"][where, pair_cols(2 * p + u)]
                r["mixed"][where, pair_cols(2 * p + u)] = jnp.where(is_pad, outs[u][b * tail : (b + 1) * tail], old)
        return carry

    lax.fori_loop(0, pairs // 2, attend_pads, 0)
    comm("plane4:2")
    have(3)

    def two(i):
        return [rows_of(2 * i), rows_of(2 * i + 1)]

    def join(i, carry):
        terms = [dot(r["mixed"][rows, :], r["W2"][...]) for rows in two(i)]
        for rows, term in zip(two(i), terms):
            middle = r["start"][rows, :] + (term + r["b2_v"][...])
            r["middle"][rows, :] = middle
            centered, rstd, mean = norm_stats(middle)
            r["stats"][2, rows, :] = mean
            r["stats"][3, rows, :] = rstd
            r["first"][rows, :] = (centered * rstd * r["g2_v"][...] + r["s2_v"][...]).astype(BF16)
        return carry

    lax.fori_loop(0, IMAGES // 2, join, 0)
    comm("plane4:3", "column5", "corner4")
    have(4)
    parts = ff // width

    def expand(i, carry):
        b, n = i // parts, lax.rem(i, parts)
        at(
            i,
            {
                0: ("plane5:0",),
                2: ("plane5:1",),
                4: ("plane5:2",),
                6: ("plane5:3",),
                8: ("corner5:01",),
                10: ("corner5:23",),
            },
        )
        rows = rows_of(b)
        cols = pl.ds(pl.multiple_of(n * width, width), width)
        pre = dot(r["first"][rows, :], r["W3"][:, cols]) + r["b3_v"][:, cols]
        hidden, slope = gelu_both(pre)
        r["hidden"][rows, cols] = hidden.astype(BF16)
        r["slope"][rows, cols] = slope.astype(BF16)
        return carry

    lax.fori_loop(0, IMAGES * parts, expand, 0)
    have(5)

    def back_hidden(i, carry):
        b, n = i // parts, lax.rem(i, parts)
        rows = rows_of(b)
        cols = pl.ds(pl.multiple_of(n * width, width), width)
        grad = dot_t(r["gres"][rows, :], r["W4"][cols, :])
        r["slope"][rows, cols] = (grad * r["slope"][rows, cols].astype(F32)).astype(BF16)
        return carry

    lax.fori_loop(0, IMAGES * parts, back_hidden, 0)

    def norm_back(grad, v, mean, rstd, gain):
        unit = (v - mean) * rstd
        scaled = grad * gain
        first = jnp.mean(scaled, axis=-1, keepdims=True)
        second = jnp.mean(scaled * unit, axis=-1, keepdims=True)
        return rstd * (scaled - first - unit * second)

    def back_join(i, carry):
        terms = [dot_t(r["slope"][rows, :], r["W3"][...]) for rows in two(i)]
        grads = []
        for rows, term in zip(two(i), terms):
            grad = norm_back(
                term, r["middle"][rows, :], r["stats"][2, rows, :], r["stats"][3, rows, :], r["g2_v"][...]
            )
            grad = r["gres"][rows, :].astype(F32) + grad
            r["gmid"][rows, :] = grad
            grads.append(grad.astype(BF16))
        for rows, grad in zip(two(i), grads):
            r["gmixed"][rows, :] = dot_t(grad, r["W2"][...]).astype(BF16)
        return carry

    lax.fori_loop(0, IMAGES // 2, back_join, 0)

    back_once = 3

    def back_attend(i, carry):
        where = [((i * back_once + u) // pairs, lax.rem(i * back_once + u, pairs)) for u in range(back_once)]

        def load(u, j):
            b, p = where[u]
            return r["qkv"][rows_of(b), part_cols(j, p)]

        def store(u, j, value):
            b, p = where[u]
            r["qkv"][rows_of(b), part_cols(j, p)] = value

        heads = [(u, h) for u in range(back_once) for h in range(2)]
        queries, keys, grads, shifted = [], [], [], []
        for u, (b, p) in enumerate(where):
            queries.append(load(u, 0))
            keys.append(load(u, 1))
            v = load(u, 2)
            go = r["gmixed"][rows_of(b), pair_cols(p)]
            inner = go.astype(F32) * r["mixed"][rows_of(b), pair_cols(p)].astype(F32)
            inner = pltpu.roll(inner, HEAD_DIM, 1).astype(BF16)
            grads.append(go)
            for h in range(2):
                own, other = lanes_of(h), lanes_of(1 - h)
                shifted.append(dot_t(go * own + inner * other, v * own - other))
        grads_t = [jnp.transpose(x) for x in grads]
        queries_t = [jnp.transpose(x) for x in queries]
        probs = [r["probs"][2 * (b * pairs + p) + h] for b, p in where for h in range(2)]
        half = [slice(0, HEAD_DIM), slice(HEAD_DIM, lanes)]
        grad_v = [dot(grads_t[u][half[h]], probs[2 * u + h]) for u, h in heads]
        ds = [(probs[n].astype(F32) * shifted[n]).astype(BF16) for n in range(len(heads))]
        for u in range(back_once):
            grad_q = dot(ds[2 * u], keys[u] * lanes_of(0)) + dot(ds[2 * u + 1], keys[u] * lanes_of(1))
            store(u, 0, (grad_q * scale).astype(BF16))
        for u in range(back_once):
            grad_k = [dot(queries_t[u][half[h]], ds[2 * u + h]) for h in range(2)]
            store(u, 1, jnp.transpose(jnp.concatenate(grad_k, axis=0).astype(BF16)))
            store(u, 2, jnp.transpose(jnp.concatenate(grad_v[2 * u : 2 * u + 2], axis=0).astype(BF16)))
        return carry

    lax.fori_loop(0, IMAGES * pairs // back_once, back_attend, 0)

    r["acc"][...] = jnp.zeros_like(r["acc"])
    heads_at = lax.broadcasted_iota(jnp.int32, (block, width), 0)

    def back_start(i, carry):
        terms = []
        for rows in two(i):
            grad = dot_t(r["qkv"][rows, 0:width], weights[0][...])
            for t in range(1, PARTS):
                grad = grad + dot_t(r["qkv"][rows, t * width : (t + 1) * width], weights[t][...])
            terms.append(grad)
        keep = lax.broadcasted_iota(jnp.int32, (head_rows, width), 0) < PROMPTS
        for rows, term in zip(two(i), terms):
            grad = norm_back(
                term, r["start"][rows, :], r["stats"][0, rows, :], r["stats"][1, rows, :], r["g1_v"][...]
            )
            grad = r["gmid"][rows, :] + grad
            top = grad[0:head_rows, :]
            r["acc"][0:head_rows, :] = r["acc"][0:head_rows, :] + jnp.where(keep, top, 0.0)
            r["first"][rows, :] = jnp.where(heads_at < PROMPTS, 0.0, grad).astype(BF16)
        return carry

    lax.fori_loop(0, IMAGES // 2, back_start, 0)

    if remote:
        red = Reduce(
            g, *(r[name] for name in ("acc", "came", "half", "plane", "line", "total")), (r["rsend_sem"], r["rrecv_sem"])
        ).steps()
    else:
        r["total"][...] = r["acc"][...]
        red = iter(range(6))
    next(red)

    def reduce_out(b):
        rows = rows_of(b)
        y = r["middle"][rows, :] + (dot(r["hidden"][rows, :], r["W4"][...]) + r["b4_v"][...])
        r["gres"][rows, :] = y.astype(BF16)

    def ship(b, src, stage, out, n):
        rows = rows_of(b)
        r[stage][rows, :] = dot(r["perm"][rows, :], r[src][...]).astype(BF16)
        pltpu.make_async_copy(r[stage].at[rows, :], r[out].at[0, rows, :], r["out_sem"].at[n, b]).start()

    def tokens_out(*blocks):
        for b in blocks:
            ship(b, "first", "gmixed", "grad_tokens", 0)

    def rows_out(*blocks):
        for b in blocks:
            ship(b, "gres", "mixed", "output", 1)

    tokens_out(0, 1)
    next(red)
    reduce_out(0)
    tokens_out(2, 3)
    next(red)
    for b in range(1, IMAGES):
        reduce_out(b)
    next(red)
    rows_out(0, 1, 2)
    next(red)
    rows_out(3)
    next(red)
    r["grad_prompt"][...] = r["total"][0:PROMPTS, :]
    for n, (stage, out) in enumerate((("gmixed", "grad_tokens"), ("mixed", "output"))):
        for b in range(IMAGES):
            rows = slice(b * block, (b + 1) * block)
            pltpu.make_async_copy(r[stage].at[rows, :], r[out].at[0, rows, :], r["out_sem"].at[n, b]).wait()
    if remote:
        g.drain()


def layer(remote, shards, args, full):
    (tokens, prompt, seg, pads, slots, g1, s1, _, b1, _, b2, g2, s2, _, b3, _, b4, cot) = args
    w1, w2, w3, w4 = full
    _, seq, width = tokens.shape
    ff = b3.shape[0]
    mult = 32 if remote else 1
    operands = [
        tokens, prompt, seg, pads, slots, g1, s1, w1, b1, w2, b2, g2, s2,
        w3, b3, w4, b4, cot,
    ]
    acc_rows = 64
    dma = pltpu.SemaphoreType.DMA
    scratch = [
        *[pltpu.VMEM((w1.shape[0] * mult, 3 * width // PARTS), BF16)] * PARTS,
        pltpu.VMEM((w2.shape[0] * mult, width), BF16),
        pltpu.VMEM((w3.shape[0] * mult, ff), BF16),
        pltpu.VMEM((w4.shape[0] * mult, width), BF16),
        pltpu.VMEM((seq, seq), BF16),
        pltpu.VMEM((seq, width), F32),
        pltpu.VMEM((seq, width), BF16),
        pltpu.VMEM((seq, 3 * width), BF16),
        pltpu.VMEM((seq, width), BF16),
        pltpu.VMEM((seq, width), F32),
        pltpu.VMEM((seq, ff), BF16),
        pltpu.VMEM((seq, ff), BF16),
        pltpu.VMEM((IMAGES * HEADS, seq // IMAGES, seq // IMAGES), BF16),
        pltpu.VMEM((seq, width), BF16),
        pltpu.VMEM((seq, width), F32),
        pltpu.VMEM((seq, width), BF16),
        pltpu.VMEM((4, seq, 1), F32),
        pltpu.VMEM((PROMPTS, width), F32),
        pltpu.VMEM((1, seq), jnp.int32),
        pltpu.VMEM((1, seq), jnp.int32),
        pltpu.VMEM((1, seq), jnp.int32),
        pltpu.VMEM((1, width), F32),
        pltpu.VMEM((1, width), F32),
        pltpu.VMEM((1, 3 * width), F32),
        pltpu.VMEM((1, width), F32),
        pltpu.VMEM((1, width), F32),
        pltpu.VMEM((1, width), F32),
        pltpu.VMEM((1, ff), F32),
        pltpu.VMEM((1, width), F32),
        pltpu.VMEM((acc_rows, width), F32),
        pltpu.VMEM((acc_rows // 2, width), F32),
        pltpu.VMEM((acc_rows // 2, width), F32),
        pltpu.VMEM((3, acc_rows // 8, width), F32),
        pltpu.VMEM((4, acc_rows // 8, width), F32),
        pltpu.VMEM((acc_rows, width), F32),
        dma((14,)),
        dma((PARTS + 3, 3)),
        dma((2, IMAGES)),
        dma((PARTS + 3, 31)),
        dma((PARTS + 3, 32)),
        dma((11,)),
        dma((11,)),
    ]
    any_spec = pl.BlockSpec(memory_space=pl.ANY)
    params = dict(vmem_limit_bytes=VMEM_LIMIT)
    if remote:
        params.update(collective_id=0, has_side_effects=True)
    return pl.pallas_call(
        functools.partial(kernel, remote, shards),
        out_shape=(
            jax.ShapeDtypeStruct(tokens.shape, BF16),
            jax.ShapeDtypeStruct(tokens.shape, BF16),
            jax.ShapeDtypeStruct((PROMPTS, width), F32),
        ),
        in_specs=[any_spec] * len(operands),
        out_specs=(any_spec, any_spec, pl.BlockSpec(memory_space=pltpu.VMEM)),
        scratch_shapes=scratch,
        compiler_params=pltpu.CompilerParams(**params),
    )(*operands)


def solution(mesh):
    devices = mesh.shape["dp"]

    def body(*args):
        weights = [args[i] for i in (7, 9, 13, 15)]
        shards = (weights[0].shape[0],) * PARTS + tuple(w.shape[0] for w in weights[1:])
        if devices == 32 and all(n % 8 == 0 for n in shards):
            output, grad_tokens, grad_prompt = layer(True, shards, args, weights)
            slots = args[4][:, :, None]
            known = jnp.where(slots <= PROMPTS, output, jnp.zeros_like(output))
            return known, jnp.where(slots < PROMPTS, jnp.zeros_like(output), grad_tokens), grad_prompt
        full = [lax.all_gather(w, "dp", axis=0, tiled=True) for w in weights]
        output, grad_tokens, grad_prompt = layer(False, shards, args, full)
        return output, grad_tokens, lax.psum(grad_prompt, "dp")

    rows = P("dp", None)
    cube = P("dp", None, None)
    in_specs = (
        cube, P(), rows, rows, rows, P(), P(), rows, P(), rows, P(), P(), P(), rows, P(), rows, P(), cube,
    )
    return jax.shard_map(body, mesh=mesh, in_specs=in_specs, out_specs=(cube, cube, P()), check_vma=False)
```

```python
import functools

import jax
import jax.numpy as jnp
from jax import lax
from jax.experimental import pallas as pl
from jax.experimental.pallas import tpu as pltpu
from jax.sharding import PartitionSpec as P

HEADS = 12
HEAD_DIM = 64
PROMPTS = 50
PATCHES = 196
IMAGES = 4
IMAGE_SLOTS = 1 + PROMPTS + PATCHES
PARTS = 3
QUARTERS = 4
EPS = 1e-06
BIG_NEGATIVE = -1e30
MESH = pl.DeviceIdType.MESH
F32 = jnp.float32
BF16 = jnp.bfloat16
DIMS = (4, 2, 2, 2)
VMEM_LIMIT = 67043328

def dot(a, b):
    return jnp.dot(a, b, preferred_element_type=F32)


def dot_t(a, b):
    return lax.dot_general(a, b, (((1,), (1,)), ((), ())), preferred_element_type=F32)


def t_dot(a, b):
    return lax.dot_general(a, b, (((0,), (0,)), ((), ())), preferred_element_type=F32)


def gelu_both(x):
    phi = 0.5 + 0.5 * lax.erf(x * 0.7071067811865476)
    density = jnp.exp2(x * (x * -0.7213475204444817))
    return x * phi, phi + x * (density * 0.3989422804014327)


class Gather:
    def __init__(self, srcs, dsts, rows, send_sem, recv_sem):
        Z, Y, X, C = DIMS
        self.src, self.dst, self.rows = srcs, dsts, rows
        self.send_sem, self.recv_sem = send_sem, recv_sem
        me = lax.axis_index("dp")
        self.me = me
        self.c = lax.rem(me, C)
        self.x = lax.rem(me // C, X)
        self.y = lax.rem(me // (C * X), Y)
        self.z = me // (C * X * Y)
        self.core = self.dev(self.z, self.y, self.x, 1 - self.c)
        self.xp = self.dev(self.z, self.y, 1 - self.x, self.c)
        self.yp = self.dev(self.z, 1 - self.y, self.x, self.c)
        self.dp = self.dev(self.z, 1 - self.y, 1 - self.x, self.c)
        self.zp = [self.dev(self.zo(j), self.y, self.x, self.c) for j in (1, 2, 3)]
        self.sent = [0] * len(rows)

    def dev(self, z, y, x, c):
        Z, Y, X, C = DIMS
        return ((z * Y + y) * X + x) * C + c

    def zo(self, j):
        return lax.rem(self.z + j, DIMS[0])

    def enter(self):
        barrier = pltpu.get_barrier_semaphore()
        peers = self.zp + [self.xp, self.yp, self.dp, self.core]
        for peer in peers:
            pl.semaphore_signal(barrier, inc=1, device_id=(peer,), device_id_type=MESH)
        pl.semaphore_wait(barrier, len(peers))

    def slot(self, k, owner):
        return self.dst[k].at[pl.ds(pl.multiple_of(owner * self.rows[k], 8), self.rows[k]), :]

    def copy(self, k, n, owner, to, src=None):
        slot = self.slot(k, owner)
        return pltpu.make_async_remote_copy(
            src_ref=slot if src is None else src,
            dst_ref=slot,
            send_sem=self.send_sem.at[k, n],
            recv_sem=self.recv_sem.at[k, owner],
            device_id=(to,),
            device_id_type=MESH,
        )

    def send(self, k, owner, to, src=None):
        self.copy(k, self.sent[k], owner, to, src).start()
        self.sent[k] += 1

    def wait(self, k, owner):
        self.copy(k, 0, owner, self.core).wait_recv()

    def line(self, k):
        for to in self.zp:
            self.send(k, self.me, to, self.src[k])

    def own(self, k):
        for to in (self.xp, self.yp, self.core):
            self.send(k, self.me, to, self.src[k])

    def column(self, k, steps=(0, 1, 2)):
        for i in steps:
            owner = self.dev(self.zo((1, 3, 2)[i]), self.y, self.x, self.c)
            self.wait(k, owner)
            for to in (self.xp, self.yp, self.core):
                self.send(k, owner, to)

    def plane(self, k, steps=(0, 1, 2, 3)):
        for i in steps:
            j = (0, 1, 3, 2)[i]
            owner = self.dev(self.zo(j), self.y, 1 - self.x, self.c)
            self.wait(k, owner)
            if i < 2:
                self.send(k, owner, self.yp)
            self.send(k, owner, self.core)
            owner = self.dev(self.zo(j), 1 - self.y, self.x, self.c)
            self.wait(k, owner)
            if i >= 2:
                self.send(k, owner, self.xp)
            self.send(k, owner, self.core)

    def corner(self, k, steps=(0, 1, 2, 3)):
        for i in steps:
            owner = self.dev(self.zo((0, 1, 3, 2)[i]), 1 - self.y, 1 - self.x, self.c)
            self.wait(k, owner)
            self.send(k, owner, self.core)

    def arrive(self, k):
        @pl.loop(0, DIMS[0] * DIMS[1] * DIMS[2])
        def _(chip):
            self.wait(k, chip * DIMS[3] + 1 - self.c)

    def drain(self):
        for k, n in enumerate(self.sent):
            for i in range(n):
                self.copy(k, i, self.me, self.core).wait_send()


class Reduce:
    def __init__(self, g, acc, came, half, plane, line, total, sems):
        self.g, self.acc, self.came, self.half, self.plane, self.line, self.total = (
            g, acc, came, half, plane, line, total
        )
        self.send_sem, self.recv_sem = sems
        self.n = 0
        rows = acc.shape[0] // 8
        self.rows = rows
        self.mine = g.c * 4 + g.y * 2 + g.x

    def tile(self, ref, i):
        return ref.at[pl.ds(pl.multiple_of(i * self.rows, 8), self.rows), :]

    def exchange(self, moves):
        copies = []
        for src, dst, to in moves:
            copies.append(
                pltpu.make_async_remote_copy(
                    src_ref=src,
                    dst_ref=dst,
                    send_sem=self.send_sem.at[self.n],
                    recv_sem=self.recv_sem.at[self.n],
                    device_id=(to,),
                    device_id_type=MESH,
                )
            )
            self.n += 1
        for copy in copies:
            copy.start()
        return copies

    def steps(self):
        g, r = self.g, self.rows
        four = 4 * r

        def halves(ref, c):
            return ref.at[pl.ds(pl.multiple_of(c * four, 8), four), :]

        one = self.exchange([(halves(self.acc, 1 - g.c), self.came.at[:, :], g.core)])
        yield
        for copy in one:
            copy.wait()
        mine = pl.ds(pl.multiple_of(g.c * four, 8), four)
        self.half[:, :] = self.acc[mine, :] + self.came[:, :]
        moves = []
        for i, (dy, dx, to) in enumerate(((0, 1, g.xp), (1, 0, g.yp), (1, 1, g.dp))):
            y = g.y if dy == 0 else 1 - g.y
            x = g.x if dx == 0 else 1 - g.x
            moves.append((self.tile(self.half, y * 2 + x), self.plane.at[i], to))
        two = self.exchange(moves)
        yield
        for copy in two:
            copy.wait()
        own = pl.ds(pl.multiple_of((g.y * 2 + g.x) * r, 8), r)
        self.line[pl.ds(g.z, 1)] = (
            (self.half[own, :] + self.plane[0]) + (self.plane[1] + self.plane[2])
        )[None]
        three = self.exchange([(self.line.at[g.z], self.line.at[g.z], to) for to in g.zp])
        yield
        for copy in three:
            copy.wait()
        total = (self.line[0] + self.line[1]) + (self.line[2] + self.line[3])
        self.total[pl.ds(pl.multiple_of(self.mine * r, 8), r), :] = total
        mine_ref = self.tile(self.total, self.mine)
        four_c = self.exchange([(mine_ref, mine_ref, to) for to in (g.xp, g.yp, g.dp)])
        yield
        for copy in four_c:
            copy.wait()
        five = self.exchange([(halves(self.total, g.c), halves(self.total, g.c), g.core)])
        yield
        for copy in five:
            copy.wait()
        yield


def kernel(remote, shards, *refs):
    names = (
        "tokens", "prompt", "seg", "pads", "slots", "g1", "s1", "w1", "b1", "w2", "b2", "g2", "s2", "w3", "b3",
        "w4", "b4", "cot", "output", "grad_tokens", "grad_prompt", "W1a", "W1b", "W1c", "W2", "W4", "W3a", "W3b", "W3c", "W3d", "perm", "start",
        "first", "qkv", "mixed", "middle", "hidden", "slope", "probs", "gres", "gmid", "gmixed",
        "stats", "prompt_v", "seg_v", "pads_v", "slots_v", "g1_v", "s1_v", "b1_v", "b2_v", "g2_v", "s2_v",
        "b3_v", "b4_v", "acc", "came", "half", "plane", "line", "total", "in_sem", "loc_sem", "out_sem",
        "send_sem", "recv_sem", "rsend_sem", "rrecv_sem",
    )
    r = dict(zip(names, refs))
    seq, width = r["start"].shape
    block = seq // IMAGES
    pads_block = block - IMAGE_SLOTS
    ff = r["hidden"].shape[1]
    pairs = HEADS // 2
    quarters = [r["W3a"], r["W3b"], r["W3c"], r["W3d"]]
    weights = [r["W1a"], r["W1b"], r["W1c"], r["W2"], r["W4"]] + quarters
    third = width // PARTS

    def rows_of(b):
        return pl.ds(pl.multiple_of(b * block, block), block)

    small = []
    for i, name in enumerate(
        ("slots", "seg", "pads", "prompt", "g1", "s1", "b1", "b2", "g2", "s2", "b3", "b4")
    ):
        dst = r[name + "_v"]
        small.append(pltpu.make_async_copy(r[name], dst if i < 4 else dst.at[0], r["in_sem"].at[i]))
    tok_in = pltpu.make_async_copy(r["tokens"].at[0], r["gmixed"], r["in_sem"].at[12])
    cot_in = pltpu.make_async_copy(r["cot"].at[0], r["mixed"], r["in_sem"].at[13])
    for copy in small + [tok_in, cot_in]:
        copy.start()
    quarter = ff // QUARTERS
    srcs = [None] * PARTS + [r["w2"], r["w4"]]
    srcs += [r["w3"].at[:, pl.ds(n * quarter, quarter)] for n in range(QUARTERS)]
    g = Gather(srcs, weights, shards, r["send_sem"], r["recv_sem"]) if remote else None
    local = []
    for k, dst in enumerate(weights):
        if remote:
            dst = g.slot(k, g.me)
        if k >= PARTS:
            local.append([pltpu.make_async_copy(srcs[k], dst, r["loc_sem"].at[k, 0])])
            continue
        local.append(
            [
                pltpu.make_async_copy(
                    r["w1"].at[:, pl.ds(j * width + k * third, third)],
                    dst.at[:, pl.ds(j * third, third)],
                    r["loc_sem"].at[k, j],
                )
                for j in range(3)
            ]
        )
    for copies in local:
        for copy in copies:
            copy.start()

    def comm(*words):
        if remote:
            for word in words:
                word, _, steps = word.partition(":")
                step = getattr(g, word[:-1])
                step(int(word[-1]), *([tuple(int(i) for i in steps)] if steps else []))

    def at(i, table):
        for step, words in table.items() if remote else ():
            pl.when(i == step)(functools.partial(comm, *words))

    def have(k):
        if k >= PARTS:
            local[k][0].wait()
        if remote:
            g.arrive(k)

    if remote:
        g.enter()
    for k in range(PARTS):
        for copy in local[k]:
            copy.wait()
        if k == 0:
            comm("line0", "own0")
    comm("line1", "own1", "line2", "own2")
    comm(*[f"line{k}" for k in range(3, len(weights))], *[f"own{k}" for k in range(3, len(weights))])

    for copy in small:
        copy.wait()
    seg = r["seg_v"][...]
    slots = r["slots_v"][...]
    is_prompt = slots < PROMPTS
    group = jnp.where(is_prompt, -1, seg)
    wanted = lax.broadcasted_iota(jnp.int32, (8, seq), 0)
    member = (wanted == group).astype(F32)
    lane = 128
    before = (
        lax.broadcasted_iota(jnp.int32, (lane, lane), 0) < lax.broadcasted_iota(jnp.int32, (lane, lane), 1)
    ).astype(F32).astype(BF16)
    counts = []
    offset = jnp.zeros((8, 1), F32)
    for i in range(seq // lane):
        part = member[:, i * lane : (i + 1) * lane]
        counts.append(dot(part.astype(BF16), before) + offset)
        offset = offset + jnp.sum(part, axis=1, keepdims=True)
    rank = jnp.sum(jnp.concatenate(counts, axis=1) * member, axis=0, keepdims=True).astype(jnp.int32)
    part_of = jnp.zeros_like(rank)
    for i in range(1, IMAGES):
        part_of = part_of + (rank >= i * pads_block).astype(jnp.int32)
    pad_dest = part_of * block + IMAGE_SLOTS + (rank - part_of * pads_block)
    image_dest = seg * block + jnp.where(is_prompt, slots, PROMPTS + rank)
    dest = jnp.where(seg < IMAGES, image_dest, pad_dest)
    live_dest = jnp.where(r["pads_v"][...] == 0, dest, -1)

    def norm_stats(v):
        mean = jnp.mean(v, axis=-1, keepdims=True)
        centered = v - mean
        return centered, lax.rsqrt(jnp.mean(centered * centered, axis=-1, keepdims=True) + EPS), mean

    tok_in.wait()
    cot_in.wait()
    head_rows = -(-PROMPTS // 8) * 8

    def place(b, carry):
        rows = rows_of(b)
        row_id = lax.broadcasted_iota(jnp.int32, (block, seq), 0) + b * block
        one_hot = (row_id == dest).astype(F32).astype(BF16)
        x = dot(one_hot, r["gmixed"][...])
        r["start"][rows, :] = x
        r["start"][pl.ds(pl.multiple_of(b * block, block), PROMPTS), :] = r["prompt_v"][...]
        centered, rstd, mean = norm_stats(r["start"][rows, :])
        r["stats"][0, rows, :] = mean
        r["stats"][1, rows, :] = rstd
        r["first"][rows, :] = (centered * rstd * r["g1_v"][...] + r["s1_v"][...]).astype(BF16)
        live = (row_id == live_dest).astype(F32).astype(BF16)
        r["gres"][rows, :] = dot(live, r["mixed"][...]).astype(BF16)
        return carry

    lax.fori_loop(0, IMAGES, place, 0)
    dest_col = jnp.transpose(jnp.broadcast_to(dest.astype(F32), (8, seq)))[:, 0:1].astype(jnp.int32)
    r["stats"][3, :, :] = dest_col.astype(F32)

    def inverse(b, carry):
        rows = rows_of(b)
        col = r["stats"][3, rows, :].astype(jnp.int32)
        r["perm"][rows, :] = (lax.broadcasted_iota(jnp.int32, (block, seq), 1) == col).astype(F32).astype(BF16)
        return carry

    lax.fori_loop(0, IMAGES, inverse, 0)

    scale = 1.0 / HEAD_DIM**0.5
    lanes = 2 * HEAD_DIM
    pairs_part = pairs // PARTS

    def pair_cols(p):
        return pl.ds(pl.multiple_of(p * lanes, lanes), lanes)

    def part_cols(j, p):
        part = p // pairs_part
        return pl.ds(pl.multiple_of(part * width + j * third + (p - part * pairs_part) * lanes, lanes), lanes)

    def project(t, table, b, carry):
        at(b, table)
        rows = rows_of(b)
        y = dot(r["first"][rows, :], weights[t][...])
        for j in range(3):
            bias = r["b1_v"][:, j * width + t * third : j * width + (t + 1) * third]
            part = (y[:, j * third : (j + 1) * third] + bias).astype(BF16)
            r["qkv"][rows, t * width + j * third : t * width + (j + 1) * third] = part * scale if j == 0 else part
        return carry

    def lanes_of(h):
        low = lax.broadcasted_iota(jnp.int32, (1, lanes), 1) < HEAD_DIM
        return (low if h == 0 else jnp.logical_not(low)).astype(F32).astype(BF16)

    def attention(load, groups, bias):
        scores, probs, outs = [], [], []
        for u in range(groups):
            q, k = load(u, 0), load(u, 1)
            scores += [dot_t(q * lanes_of(h), k) + bias for h in range(2)]
        for s in scores:
            e = jnp.exp(s - jnp.max(s, axis=-1, keepdims=True))
            probs.append((e * (1.0 / jnp.sum(e, axis=-1, keepdims=True))).astype(BF16))
        for u in range(groups):
            v = load(u, 2)
            out = dot(probs[2 * u], v * lanes_of(0)) + dot(probs[2 * u + 1], v * lanes_of(1))
            outs.append(out.astype(BF16))
        return probs, outs

    def bias_of(shape, bad):
        return jnp.where(bad(lax.broadcasted_iota(jnp.int32, shape, 1)), BIG_NEGATIVE, 0.0)

    at_once = 4

    def pair_of(t, i):
        return i // pairs_part, t * pairs_part + lax.rem(i, pairs_part)

    def attend(t, table, i, carry):
        at(i, table)
        where = [pair_of(t, i * at_once + u) for u in range(at_once)]

        def load(u, j):
            b, p = where[u]
            return r["qkv"][rows_of(b), part_cols(j, p)]

        probs, outs = attention(load, at_once, bias_of((1, block), lambda col: col >= IMAGE_SLOTS))
        for u, (b, p) in enumerate(where):
            for h in range(2):
                r["probs"][2 * (b * pairs + p) + h] = probs[2 * u + h]
            r["mixed"][rows_of(b), pair_cols(p)] = outs[u]
        return carry

    tables = (
        ({2: ("plane3:01",)}, {0: ("plane3:23",), 1: ("corner2",)}),
        ({2: ("column4:0",)}, {0: ("column4:1",), 1: ("column4:2", "corner3")}),
        ({2: ("plane4:0",)}, {0: ("column5",), 1: ("plane4:1",)}),
    )
    comm("column0", "column1", "plane0", "column2", "plane1", "corner0", "column3", "plane2", "corner1")
    for t in range(PARTS):
        have(t)
        lax.fori_loop(0, IMAGES, functools.partial(project, t, tables[t][0]), 0)
        lax.fori_loop(0, IMAGES * pairs_part // at_once, functools.partial(attend, t, tables[t][1]), 0)

    tail = 16
    group_rows = IMAGES * tail

    def attend_pads(p, carry):
        def load(u, j):
            return jnp.concatenate(
                [
                    r["qkv"][b * block + block - tail : (b + 1) * block, part_cols(j, 2 * p + u)]
                    for b in range(IMAGES)
                ],
                axis=0,
            )

        bias = bias_of((1, group_rows), lambda col: lax.rem(col, tail) < tail - pads_block)
        outs = attention(load, 2, bias)[1]
        is_pad = lax.broadcasted_iota(jnp.int32, (tail, lanes), 0) >= tail - pads_block
        for u in range(2):
            for b in range(IMAGES):
                where = slice(b * block + block - tail, (b + 1) * block)
                old = r["mixed"][where, pair_cols(2 * p + u)]
                r["mixed"][where, pair_cols(2 * p + u)] = jnp.where(is_pad, outs[u][b * tail : (b + 1) * tail], old)
        return carry

    lax.fori_loop(0, pairs // 2, attend_pads, 0)
    comm("plane4:2")
    have(3)

    def two(i):
        return [rows_of(2 * i), rows_of(2 * i + 1)]

    def join(i, carry):
        terms = [dot(r["mixed"][rows, :], r["W2"][...]) for rows in two(i)]
        for rows, term in zip(two(i), terms):
            middle = r["start"][rows, :] + (term + r["b2_v"][...])
            r["middle"][rows, :] = middle
            centered, rstd, mean = norm_stats(middle)
            r["stats"][2, rows, :] = mean
            r["stats"][3, rows, :] = rstd
            r["first"][rows, :] = (centered * rstd * r["g2_v"][...] + r["s2_v"][...]).astype(BF16)
        return carry

    lax.fori_loop(0, IMAGES // 2, join, 0)
    comm("plane4:3", "column6", "plane5", "corner4")
    have(4)
    parts = ff // width

    def back_hidden(i, carry):
        b, n = i // parts, lax.rem(i, parts)
        at(
            i,
            {
                0: ("column7",),
                2: ("plane6:01",),
                4: ("plane6:23",),
                6: ("corner5",),
                8: ("column8",),
                11: ("plane7:01",),
                14: ("plane7:23",),
            },
        )
        rows = rows_of(b)
        cols = pl.ds(pl.multiple_of(n * width, width), width)
        r["slope"][rows, cols] = dot_t(r["gres"][rows, :], r["W4"][cols, :]).astype(BF16)
        return carry

    lax.fori_loop(0, IMAGES * parts, back_hidden, 0)

    def feed(n, table, i, carry):
        at(i, table)
        cols = slice(n * quarter, (n + 1) * quarter)
        pres = [dot(r["first"][rows, :], quarters[n][...]) + r["b3_v"][:, cols] for rows in two(i)]
        grads = []
        for rows, pre in zip(two(i), pres):
            hidden, slope = gelu_both(pre)
            r["hidden"][rows, cols] = hidden.astype(BF16)
            grads.append((r["slope"][rows, cols].astype(F32) * slope).astype(BF16))
        for rows, grad in zip(two(i), grads):
            term = dot_t(grad, quarters[n][...])
            r["gmid"][rows, :] = term if n == 0 else r["gmid"][rows, :] + term
        return carry

    feed_tables = (
        {0: ("corner6",), 1: ("plane8:01",)},
        {0: ("plane8:23",), 1: ("corner7",)},
        {1: ("corner8",)},
        {},
    )
    for n in range(QUARTERS):
        have(PARTS + 2 + n)
        lax.fori_loop(0, IMAGES // 2, functools.partial(feed, n, feed_tables[n]), 0)

    def norm_back(grad, v, mean, rstd, gain):
        unit = (v - mean) * rstd
        scaled = grad * gain
        first = jnp.mean(scaled, axis=-1, keepdims=True)
        second = jnp.mean(scaled * unit, axis=-1, keepdims=True)
        return rstd * (scaled - first - unit * second)

    def back_join(i, carry):
        terms = [r["gmid"][rows, :] for rows in two(i)]
        grads = []
        for rows, term in zip(two(i), terms):
            grad = norm_back(
                term, r["middle"][rows, :], r["stats"][2, rows, :], r["stats"][3, rows, :], r["g2_v"][...]
            )
            grad = r["gres"][rows, :].astype(F32) + grad
            r["gmid"][rows, :] = grad
            grads.append(grad.astype(BF16))
        for rows, grad in zip(two(i), grads):
            r["gmixed"][rows, :] = dot_t(grad, r["W2"][...]).astype(BF16)
        return carry

    lax.fori_loop(0, IMAGES // 2, back_join, 0)

    back_once = 3

    def back_attend(i, carry):
        where = [((i * back_once + u) // pairs, lax.rem(i * back_once + u, pairs)) for u in range(back_once)]

        def load(u, j):
            b, p = where[u]
            return r["qkv"][rows_of(b), part_cols(j, p)]

        def store(u, j, value):
            b, p = where[u]
            r["qkv"][rows_of(b), part_cols(j, p)] = value

        heads = [(u, h) for u in range(back_once) for h in range(2)]
        queries, keys, grads, shifted = [], [], [], []
        for u, (b, p) in enumerate(where):
            queries.append(load(u, 0))
            keys.append(load(u, 1))
            v = load(u, 2)
            go = r["gmixed"][rows_of(b), pair_cols(p)]
            inner = go.astype(F32) * r["mixed"][rows_of(b), pair_cols(p)].astype(F32)
            inner = pltpu.roll(inner, HEAD_DIM, 1).astype(BF16)
            grads.append(go)
            for h in range(2):
                own, other = lanes_of(h), lanes_of(1 - h)
                shifted.append(dot_t(go * own + inner * other, v * own - other))
        grads_t = [jnp.transpose(x) for x in grads]
        queries_t = [jnp.transpose(x) for x in queries]
        probs = [r["probs"][2 * (b * pairs + p) + h] for b, p in where for h in range(2)]
        half = [slice(0, HEAD_DIM), slice(HEAD_DIM, lanes)]
        grad_v = [dot(grads_t[u][half[h]], probs[2 * u + h]) for u, h in heads]
        ds = [(probs[n].astype(F32) * shifted[n]).astype(BF16) for n in range(len(heads))]
        for u in range(back_once):
            grad_q = dot(ds[2 * u], keys[u] * lanes_of(0)) + dot(ds[2 * u + 1], keys[u] * lanes_of(1))
            store(u, 0, (grad_q * scale).astype(BF16))
        for u in range(back_once):
            grad_k = [dot(queries_t[u][half[h]], ds[2 * u + h]) for h in range(2)]
            store(u, 1, jnp.transpose(jnp.concatenate(grad_k, axis=0).astype(BF16)))
            store(u, 2, jnp.transpose(jnp.concatenate(grad_v[2 * u : 2 * u + 2], axis=0).astype(BF16)))
        return carry

    lax.fori_loop(0, IMAGES * pairs // back_once, back_attend, 0)

    r["acc"][...] = jnp.zeros_like(r["acc"])
    heads_at = lax.broadcasted_iota(jnp.int32, (block, width), 0)

    def back_start(i, carry):
        terms = []
        for rows in two(i):
            grad = dot_t(r["qkv"][rows, 0:width], weights[0][...])
            for t in range(1, PARTS):
                grad = grad + dot_t(r["qkv"][rows, t * width : (t + 1) * width], weights[t][...])
            terms.append(grad)
        keep = lax.broadcasted_iota(jnp.int32, (head_rows, width), 0) < PROMPTS
        for rows, term in zip(two(i), terms):
            grad = norm_back(
                term, r["start"][rows, :], r["stats"][0, rows, :], r["stats"][1, rows, :], r["g1_v"][...]
            )
            grad = r["gmid"][rows, :] + grad
            top = grad[0:head_rows, :]
            r["acc"][0:head_rows, :] = r["acc"][0:head_rows, :] + jnp.where(keep, top, 0.0)
            r["first"][rows, :] = jnp.where(heads_at < PROMPTS, 0.0, grad).astype(BF16)
        return carry

    lax.fori_loop(0, IMAGES // 2, back_start, 0)

    if remote:
        red = Reduce(
            g, *(r[name] for name in ("acc", "came", "half", "plane", "line", "total")), (r["rsend_sem"], r["rrecv_sem"])
        ).steps()
    else:
        r["total"][...] = r["acc"][...]
        red = iter(range(6))
    next(red)

    def reduce_out(b):
        rows = rows_of(b)
        y = r["middle"][rows, :] + (dot(r["hidden"][rows, :], r["W4"][...]) + r["b4_v"][...])
        r["gres"][rows, :] = y.astype(BF16)

    def ship(b, src, stage, out, n):
        rows = rows_of(b)
        r[stage][rows, :] = dot(r["perm"][rows, :], r[src][...]).astype(BF16)
        pltpu.make_async_copy(r[stage].at[rows, :], r[out].at[0, rows, :], r["out_sem"].at[n, b]).start()

    def tokens_out(*blocks):
        for b in blocks:
            ship(b, "first", "gmixed", "grad_tokens", 0)

    def rows_out(*blocks):
        for b in blocks:
            ship(b, "gres", "mixed", "output", 1)

    tokens_out(0, 1)
    next(red)
    reduce_out(0)
    tokens_out(2, 3)
    next(red)
    for b in range(1, IMAGES):
        reduce_out(b)
    next(red)
    rows_out(0, 1, 2)
    next(red)
    rows_out(3)
    next(red)
    r["grad_prompt"][...] = r["total"][0:PROMPTS, :]
    for n, (stage, out) in enumerate((("gmixed", "grad_tokens"), ("mixed", "output"))):
        for b in range(IMAGES):
            rows = slice(b * block, (b + 1) * block)
            pltpu.make_async_copy(r[stage].at[rows, :], r[out].at[0, rows, :], r["out_sem"].at[n, b]).wait()
    if remote:
        g.drain()


def layer(remote, shards, args, full):
    (tokens, prompt, seg, pads, slots, g1, s1, _, b1, _, b2, g2, s2, _, b3, _, b4, cot) = args
    w1, w2, w3, w4 = full
    _, seq, width = tokens.shape
    ff = b3.shape[0]
    mult = 32 if remote else 1
    operands = [
        tokens, prompt, seg, pads, slots, g1, s1, w1, b1, w2, b2, g2, s2,
        w3, b3, w4, b4, cot,
    ]
    acc_rows = 64
    dma = pltpu.SemaphoreType.DMA
    scratch = [
        *[pltpu.VMEM((w1.shape[0] * mult, 3 * width // PARTS), BF16)] * PARTS,
        pltpu.VMEM((w2.shape[0] * mult, width), BF16),
        pltpu.VMEM((w4.shape[0] * mult, width), BF16),
        *[pltpu.VMEM((w3.shape[0] * mult, ff // QUARTERS), BF16)] * QUARTERS,
        pltpu.VMEM((seq, seq), BF16),
        pltpu.VMEM((seq, width), F32),
        pltpu.VMEM((seq, width), BF16),
        pltpu.VMEM((seq, 3 * width), BF16),
        pltpu.VMEM((seq, width), BF16),
        pltpu.VMEM((seq, width), F32),
        pltpu.VMEM((seq, ff), BF16),
        pltpu.VMEM((seq, ff), BF16),
        pltpu.VMEM((IMAGES * HEADS, seq // IMAGES, seq // IMAGES), BF16),
        pltpu.VMEM((seq, width), BF16),
        pltpu.VMEM((seq, width), F32),
        pltpu.VMEM((seq, width), BF16),
        pltpu.VMEM((4, seq, 1), F32),
        pltpu.VMEM((PROMPTS, width), F32),
        pltpu.VMEM((1, seq), jnp.int32),
        pltpu.VMEM((1, seq), jnp.int32),
        pltpu.VMEM((1, seq), jnp.int32),
        pltpu.VMEM((1, width), F32),
        pltpu.VMEM((1, width), F32),
        pltpu.VMEM((1, 3 * width), F32),
        pltpu.VMEM((1, width), F32),
        pltpu.VMEM((1, width), F32),
        pltpu.VMEM((1, width), F32),
        pltpu.VMEM((1, ff), F32),
        pltpu.VMEM((1, width), F32),
        pltpu.VMEM((acc_rows, width), F32),
        pltpu.VMEM((acc_rows // 2, width), F32),
        pltpu.VMEM((acc_rows // 2, width), F32),
        pltpu.VMEM((3, acc_rows // 8, width), F32),
        pltpu.VMEM((4, acc_rows // 8, width), F32),
        pltpu.VMEM((acc_rows, width), F32),
        dma((14,)),
        dma((PARTS + 2 + QUARTERS, 3)),
        dma((2, IMAGES)),
        dma((PARTS + 2 + QUARTERS, 31)),
        dma((PARTS + 2 + QUARTERS, 32)),
        dma((11,)),
        dma((11,)),
    ]
    any_spec = pl.BlockSpec(memory_space=pl.ANY)
    params = dict(vmem_limit_bytes=VMEM_LIMIT)
    if remote:
        params.update(collective_id=0, has_side_effects=True)
    return pl.pallas_call(
        functools.partial(kernel, remote, shards),
        out_shape=(
            jax.ShapeDtypeStruct(tokens.shape, BF16),
            jax.ShapeDtypeStruct(tokens.shape, BF16),
            jax.ShapeDtypeStruct((PROMPTS, width), F32),
        ),
        in_specs=[any_spec] * len(operands),
        out_specs=(any_spec, any_spec, pl.BlockSpec(memory_space=pltpu.VMEM)),
        scratch_shapes=scratch,
        compiler_params=pltpu.CompilerParams(**params),
    )(*operands)


def solution(mesh):
    devices = mesh.shape["dp"]

    def body(*args):
        weights = [args[i] for i in (7, 9, 13, 15)]
        depth = [w.shape[0] for w in weights]
        shards = (depth[0],) * PARTS + (depth[1], depth[3]) + (depth[2],) * QUARTERS
        if devices == 32 and all(n % 8 == 0 for n in shards):
            output, grad_tokens, grad_prompt = layer(True, shards, args, weights)
            slots = args[4][:, :, None]
            known = jnp.where(slots <= PROMPTS, output, jnp.zeros_like(output))
            return known, jnp.where(slots < PROMPTS, jnp.zeros_like(output), grad_tokens), grad_prompt
        full = [lax.all_gather(w, "dp", axis=0, tiled=True) for w in weights]
        output, grad_tokens, grad_prompt = layer(False, shards, args, full)
        return output, grad_tokens, lax.psum(grad_prompt, "dp")

    rows = P("dp", None)
    cube = P("dp", None, None)
    in_specs = (
        cube, P(), rows, rows, rows, P(), P(), rows, P(), rows, P(), P(), P(), rows, P(), rows, P(), cube,
    )
    return jax.shard_map(body, mesh=mesh, in_specs=in_specs, out_specs=(cube, cube, P()), check_vma=False)
```
